32 devices in a mesh: dp: 4 (over y, x), expert: 8 (over z, core).
Axes of the slice: x: 2, y: 2, z: 4, core: 2. Of those that a mesh axis runs over, the one named last changes fastest.
Arguments:
- tokens: bfloat16 [4096, 1536], P('expert'), may hold values from -6 to 6
- past_len: int32 [32], P('expert'), may hold values from 1 to 4608
- cache_keys: bfloat16 [32, 4608, 512], P('expert', None, 'dp'), may hold values from -32 to 32
- cache_values: bfloat16 [32, 4608, 512], P('expert', None, 'dp'), may hold values from -6 to 6
- attn_gain: float32 [1536], replicated, may hold values from 0.1 to 1.9
- w_query: bfloat16 [1536, 1536], P(None, 'dp'), may hold values from -3 to 3
- w_key: bfloat16 [1536, 512], P(None, 'dp'), may hold values from -0.15625 to 0.15625
- w_value: bfloat16 [1536, 512], P(None, 'dp'), may hold values from -0.15625 to 0.15625
- w_out: bfloat16 [1536, 1536], P('dp'), may hold values from -0.15625 to 0.15625
- moe_gain: float32 [1536], replicated, may hold values from 0.1 to 1.9
- router: bfloat16 [1536, 40], replicated, may hold values from -16 to 16
- expert_in: bfloat16 [64, 1536, 1024], P('expert'), may hold values from -0.15625 to 0.15625
- expert_out: bfloat16 [64, 512, 1536], P('expert'), may hold values from -1 to 1
- final_gain: float32 [1536], replicated, may hold values from 0.1 to 1.9
- slot_owner: int32 [64], replicated, may hold values from 0 to 39, as said below
- routes: int32 [4096, 8], P(('expert', 'dp')), may hold values from 0 to 39, all different within a row; in each aligned block of 128 rows (0 to 127, 128 to 255, ...) at most 40 rows name the same one
- split_pick: int32 [4096, 8], P(('expert', 'dp')), may hold values from 0 to 2519
Outputs:
- output: bfloat16 [4096, 1536], P(('expert', 'dp'))
The draws below stay inside these ranges and needn't reach their ends.
Inputs may be any that keep to these rules, and one draw needn't show every extreme that they name: `routes`: each row names 8 different experts; at most 40 rows of one device name one expert, a bound that some block reaches. `slot_owner`: every expert is served by at least one slot.
All inputs are finite; a program needn't handle non-finite values.
Results may differ from the reference program's by a relative error of at most 0.025.
Values may be sent and summed in bfloat16 or wider, within the bound.
A program may use at most 128 MiB of HBM per device.

```python
import math
import jax
import jax.numpy as jnp
import numpy as np
from jax import lax

D = 1536
HEADS = 24
KVH = 8
HD = 64
EXPERTS = 40
FF = 512
TOPK = 8
SINK = 4
WINDOW = 4096
CAP = 4608
QPR = 128
TOK_DEV = 128
TOKENS = 4096
REQS = 32
SLOTS = 64
MOST = 40


def draw_w_query(key, part):
    noise = jnp.clip(jax.random.normal(jax.random.fold_in(key, 11), (D, HEADS * HD), jnp.float32), -6.0, 6.0) / math.sqrt(D)
    return noise.astype(jnp.bfloat16)


def draw_cache_keys(key, part):
    noise = jnp.clip(jax.random.normal(jax.random.fold_in(key, 21), (REQS, CAP, KVH * HD), jnp.float32), -6.0, 6.0)
    return noise.astype(jnp.bfloat16)


def draw_router(key, part):
    noise = jnp.clip(jax.random.normal(jax.random.fold_in(key, 31), (D, EXPERTS), jnp.float32), -6.0, 6.0)
    values = 0.35 * noise / math.sqrt(D)
    return values.astype(jnp.bfloat16)


def draw_slot_owner(key, part):
    order = jax.random.permutation(jax.random.fold_in(key, 41), SLOTS)
    extra = jax.random.randint(jax.random.fold_in(key, 42), (SLOTS,), 0, EXPERTS)
    return jnp.where(order < EXPERTS, order, extra).astype(jnp.int32)


def with_ends(array, own_key, smallest, top_value):
    dims = array.shape
    place = [jax.random.randint(jax.random.fold_in(own_key, axis), (), 0, dims[axis]) for axis in range(len(dims))]
    array = array.at[tuple(place)].set(smallest)
    longest = dims.index(max(dims))
    place[longest] = (place[longest] + 1) % dims[longest]
    return array.at[tuple(place)].set(top_value)


def levels(stream_key, shape, cuts, smallest, top_value):
    level, own = 1.0, jax.random.fold_in(stream_key, 6)
    for dim, parts in cuts:
        steps = jnp.exp(jax.random.uniform(jax.random.fold_in(own, dim), (parts,), jnp.float32, smallest / len(cuts), top_value / len(cuts)))
        level = level * jnp.repeat(steps, shape[dim] // parts).reshape([-1 if axis == dim else 1 for axis in range(len(shape))])
    return level


def routed_block(key, own, number, rows, amount, top, most, lean):
    ranking = jax.random.permutation(key, amount)
    packed, ordinary = load_shares(amount, rows * top, most, lean, True), load_shares(amount, rows * top, most, lean, False)
    places = jnp.arange(amount)

    def named(lengths, offset_by):
        used = int((lengths > 0).sum())
        fixed = max(1, used // 4)
        moved = fixed + (places - fixed + offset_by * (used - fixed)) % max(1, amount - fixed)
        return jnp.zeros((amount,), jnp.int32).at[ranking[jnp.where(places < fixed, places, moved)]].set(jnp.asarray(lengths, jnp.int32))

    lengths = jnp.where(number % 4 == 0, named(packed, number // 4), named(ordinary, number - number // 4 - 1))
    mixed = jax.random.permutation(jax.random.fold_in(own, 3), amount)
    giver, sink = mixed[0:amount // 2 * 2:2], mixed[1:amount // 2 * 2:2]
    margin = jnp.minimum(lengths[giver] - 1, most - lengths[sink]) // 2
    margin = jnp.where((giver == ranking[0]) | (sink == ranking[0]) | (lengths[sink] == 0), 0, jnp.maximum(margin, 0))
    moved = jax.random.randint(jax.random.fold_in(own, 4), (amount // 2,), 0, 1 << 20) % (margin + 1)
    lengths = lengths.at[giver].add(-moved).at[sink].add(moved)
    members = jnp.searchsorted(jnp.cumsum(lengths), jnp.arange(rows * top), side="right").astype(jnp.int32)
    grid = members.reshape(top, rows).T
    grid = grid[jax.random.permutation(jax.random.fold_in(own, 1), rows)]
    offset_by = jax.random.randint(jax.random.fold_in(own, 2), (rows, 1), 0, top)
    return jnp.take_along_axis(grid, (jnp.arange(top)[None, :] + offset_by) % top, axis=1)


def load_shares(number_of, total, bound, slope, full):
    portions = [(1 << 20) // math.isqrt(rank ** slope) + 1 for rank in range(1, number_of + 1)]
    largest = bound if full else min(bound, max(-(-total // number_of), total * portions[0] // sum(portions)))
    least = 1 if total - largest >= number_of - 1 else 0
    given, spare = [largest] + [least] * (number_of - 1), total - largest - least * (number_of - 1)
    while spare > 0:
        movable = [i for i in range(1, number_of) if given[i] < largest] or [i for i in range(1, number_of) if given[i] < bound]
        pool, budget = sum([portions[i] for i in movable]), spare
        for i in movable:
            more = min(bound - given[i], max(1, budget * portions[i] // pool), spare)
            given[i] = given[i] + more
            spare = spare - more
    return np.array(given)


def scatter_about(key, dims, deviation, bound, shards=(), kind=jnp.bfloat16):
    loudness = levels(key, dims, shards, -0.22, 0.18) if shards else 1.0
    entries = jax.random.normal(key, dims, jnp.float32) * deviation * loudness
    return jnp.minimum(jnp.maximum(entries, -bound), bound).astype(kind)


def setup_inputs(seed: int = 0) -> dict:
    seeds = jax.random.split(jax.random.key(seed), 18)
    tokens = scatter_about(seeds[0], (TOKENS, D), 1.0, 6.0, ((0, 8),))
    past_len = with_ends(jax.random.randint(seeds[1], (REQS,), 1, CAP + 1), jax.random.fold_in(seeds[1], 1), 1, CAP).astype(jnp.int32)
    cache_keys = draw_cache_keys(jax.random.fold_in(seeds[17], 71), 0)
    cache_values = scatter_about(seeds[3], (REQS, CAP, KVH * HD), 1.0, 6.0, ((0, 8), (2, 4)))
    attn_gain = jnp.clip(1.0 + 0.18 * jax.random.normal(seeds[4], (D,), jnp.float32), 0.1, 1.9)
    w_query = draw_w_query(jax.random.fold_in(seeds[17], 71), 0)
    w_key = scatter_about(seeds[6], (D, KVH * HD), D ** -0.5, 0.15625, ((1, 4),))
    w_value = scatter_about(seeds[7], (D, KVH * HD), D ** -0.5, 0.15625, ((1, 4),))
    w_out = scatter_about(seeds[8], (HEADS * HD, D), (HEADS * HD) ** -0.5, 0.15625, ((0, 4),))
    moe_gain = jnp.clip(1.0 + 0.18 * jax.random.normal(seeds[9], (D,), jnp.float32), 0.1, 1.9)
    router = draw_router(jax.random.fold_in(seeds[17], 71), 0)
    expert_in = scatter_about(seeds[11], (SLOTS, D, 2 * FF), D ** -0.5, 0.15625, ((0, 8),))
    expert_out = scatter_about(seeds[12], (SLOTS, FF, D), (FF // 16) ** -0.5, 1.0, ((0, 8),))
    final_gain = jnp.clip(1.0 + 0.18 * jax.random.normal(seeds[13], (D,), jnp.float32), 0.1, 1.9)
    slot_owner = draw_slot_owner(jax.random.fold_in(seeds[17], 71), 0)
    routes_keys = jax.random.split(jax.random.fold_in(seeds[15], 1), TOKENS // TOK_DEV)
    routes_turns = jax.random.permutation(jax.random.fold_in(seeds[15], 3), TOKENS // TOK_DEV)
    routes = jax.vmap(lambda own, number: routed_block(jax.random.fold_in(seeds[15], 2), own, number, TOK_DEV, EXPERTS, TOPK, MOST, 2))(routes_keys, routes_turns).reshape((TOKENS, TOPK))
    split_pick = with_ends(jax.random.randint(seeds[16], (TOKENS, TOPK), 0, 2520), jax.random.fold_in(seeds[16], 1), 0, 2519).astype(jnp.int32)
    return {"tokens": tokens, "past_len": past_len, "cache_keys": cache_keys, "cache_values": cache_values, "attn_gain": attn_gain, "w_query": w_query, "w_key": w_key, "w_value": w_value, "w_out": w_out, "moe_gain": moe_gain, "router": router, "expert_in": expert_in, "expert_out": expert_out, "final_gain": final_gain, "slot_owner": slot_owner, "routes": routes, "split_pick": split_pick}


epsilon = 1e-05

def rms_scale(values, gain):
    widened = values.astype(jnp.float32)
    mean_square = lax.optimization_barrier(jnp.mean(widened * widened, axis=-1, keepdims=True))
    return widened * lax.rsqrt(mean_square + epsilon) * gain.astype(jnp.float32)

def attend_request(item):
    queries, keys_new, values_new, keys_past, values_past, length = item
    share_count = HEADS // KVH
    query_all = queries.astype(jnp.float32).reshape(QPR, KVH, share_count, HD)
    keys_all = jnp.concatenate([keys_past.reshape(CAP, KVH, HD), keys_new.reshape(QPR, KVH, HD)], 0).astype(jnp.float32)
    values_all = jnp.concatenate([values_past.reshape(CAP, KVH, HD), values_new.reshape(QPR, KVH, HD)], 0).astype(jnp.float32)
    scores = jnp.einsum('qkgd,pkd->kgqp', query_all, keys_all) * HD ** (-0.5)
    position = jnp.arange(QPR, dtype=jnp.int32)[:, None]
    slot_place = jnp.arange(CAP, dtype=jnp.int32)[None, :]
    live_past = (slot_place < length) & ((slot_place < SINK) | (slot_place >= length + position - WINDOW + 1))
    live_new = jnp.arange(QPR, dtype=jnp.int32)[None, :] <= position
    live = jnp.concatenate([live_past, live_new], 1)
    masked = jnp.where(live, scores, -jnp.inf)
    highest = lax.optimization_barrier(jnp.max(masked, axis=-1, keepdims=True))
    weights = jnp.where(live, jnp.exp(masked - highest), 0.0)
    totals = lax.optimization_barrier(jnp.sum(weights, axis=-1, keepdims=True))
    rounded = lax.optimization_barrier(weights.astype(jnp.bfloat16))
    summed = jnp.einsum('kgqp,pkd->kgqd', rounded.astype(jnp.float32), values_all) / totals
    return summed.transpose(2, 0, 1, 3).reshape(QPR, HEADS * HD).astype(jnp.bfloat16)

def reference(tokens, past_len, cache_keys, cache_values, attn_gain, w_query, w_key, w_value, w_out, moe_gain, router, expert_in, expert_out, final_gain, slot_owner, routes, split_pick):
    normed = rms_scale(tokens, attn_gain).astype(jnp.bfloat16)
    queries = jnp.dot(normed, w_query, preferred_element_type=jnp.float32).astype(jnp.bfloat16)
    keys_new = jnp.dot(normed, w_key, preferred_element_type=jnp.float32).astype(jnp.bfloat16)
    values_new = jnp.dot(normed, w_value, preferred_element_type=jnp.float32).astype(jnp.bfloat16)
    heads = lax.map(attend_request, (queries.reshape(REQS, QPR, HEADS * HD), keys_new.reshape(REQS, QPR, KVH * HD), values_new.reshape(REQS, QPR, KVH * HD), cache_keys, cache_values, past_len))
    heads = heads.reshape(TOKENS, HEADS * HD)
    stream = tokens.astype(jnp.float32) + jnp.dot(heads, w_out, preferred_element_type=jnp.float32)
    moe_in = rms_scale(stream, moe_gain).astype(jnp.bfloat16)
    logits = jnp.dot(moe_in, router, preferred_element_type=jnp.float32)
    chosen = jnp.take_along_axis(logits, routes, axis=1)
    gates = jax.nn.softmax(chosen, axis=-1)
    slot_ids = jnp.arange(SLOTS, dtype=jnp.int32)
    same_owner = slot_owner[:, None] == slot_owner[None, :]
    slot_rank = lax.optimization_barrier(jnp.sum((same_owner & (slot_ids[None, :] < slot_ids[:, None])).astype(jnp.int32), axis=1))
    serving = slot_owner[None, None, :] == routes[:, :, None]
    replicas = lax.optimization_barrier(jnp.sum(serving.astype(jnp.int32), axis=-1))
    wanted = split_pick % replicas
    target = lax.optimization_barrier(jnp.sum(jnp.where(serving & (slot_rank[None, None, :] == wanted[:, :, None]), slot_ids[None, None, :], 0), axis=-1)).astype(jnp.int32)
    route_count = TOKENS * TOPK
    flat_slot = target.reshape(route_count)
    tile_rows = 128
    tiles = (route_count + tile_rows - 1) // tile_rows + SLOTS
    counts = lax.optimization_barrier(jnp.sum((flat_slot[:, None] == slot_ids[None, :]).astype(jnp.int32), axis=0))
    padded = (counts + tile_rows - 1) // tile_rows * tile_rows
    starts = jnp.cumsum(padded) - padded
    firsts = jnp.cumsum(counts) - counts
    order = jnp.argsort(flat_slot, stable=True).astype(jnp.int32)
    sorted_slot = flat_slot[order]
    placed = (starts[sorted_slot] + jnp.arange(route_count, dtype=jnp.int32) - firsts[sorted_slot]).astype(jnp.int32)
    location = jnp.zeros((route_count,), jnp.int32).at[order].set(placed)
    source_index = (jnp.arange(route_count, dtype=jnp.int32) // TOPK).astype(jnp.int32)
    buffer = jnp.zeros((tiles * tile_rows, D), jnp.bfloat16).at[location].set(moe_in[source_index])
    ends = starts + padded
    tile_start = jnp.arange(tiles, dtype=jnp.int32) * tile_rows
    tile_slot = jnp.minimum(lax.optimization_barrier(jnp.sum((ends[None, :] <= tile_start[:, None]).astype(jnp.int32), axis=1)), SLOTS - 1).astype(jnp.int32)

    def run_tile(item):
        tile_in, which = item
        gate_up = jnp.dot(tile_in, expert_in[which], preferred_element_type=jnp.float32)
        activation = (jax.nn.silu(gate_up[:, :FF]) * gate_up[:, FF:]).astype(jnp.bfloat16)
        return jnp.dot(activation, expert_out[which], preferred_element_type=jnp.float32).astype(jnp.bfloat16)
    outputs = lax.map(run_tile, (buffer.reshape(tiles, tile_rows, D), tile_slot)).reshape(tiles * tile_rows, D)
    expert_rows = outputs[location].reshape(TOKENS, TOPK, D)
    combined = stream + lax.optimization_barrier(jnp.sum(gates[:, :, None] * expert_rows.astype(jnp.float32), axis=1))
    return rms_scale(combined, final_gain).astype(jnp.bfloat16)
```

```python
import functools
import math

import jax
import jax.numpy as jnp
from jax import lax
from jax.experimental import pallas as pl
from jax.experimental.pallas import tpu as pltpu
from jax.sharding import PartitionSpec as P

HD = 64
SINK = 4
WINDOW = 4096
MOST = 40

epsilon = 1e-05
neg_large = -1e30


def rms_scale(values, gain):
    widened = values.astype(jnp.float32)
    mean_square = jnp.mean(widened * widened, axis=-1, keepdims=True)
    return widened * lax.rsqrt(mean_square + epsilon) * gain


def mm(a, b):
    return jnp.dot(a, b, preferred_element_type=jnp.float32)


def attend_kernel(
    key_block, len_ref, tok_ref, gain_ref, wq_ref, wk_ref, wv_ref, wo_ref, kc_ref, vc_ref,
    out_ref, qt_ref, top_ref, total_ref, acc_ref,
):
    length = len_ref[pl.program_id(0)]
    rows = tok_ref.shape[0]
    heads = wq_ref.shape[1] // HD
    kv_local = wk_ref.shape[1] // HD
    share = heads // kv_local
    columns = heads * rows
    normed = rms_scale(tok_ref[...], gain_ref[...]).astype(jnp.bfloat16)
    queries = mm(normed, wq_ref[...]).astype(jnp.bfloat16).astype(jnp.float32) * HD ** (-0.5)
    queries_t = queries.T.astype(jnp.bfloat16)
    qt_ref[...] = jnp.zeros_like(qt_ref)
    for h in range(heads):
        kv = h // share
        qt_ref[kv * HD : (kv + 1) * HD, h * rows : (h + 1) * rows] = queries_t[h * HD : (h + 1) * HD, :]
    keys_new = mm(normed, wk_ref[...]).astype(jnp.bfloat16)
    values_new = mm(normed, wv_ref[...]).astype(jnp.bfloat16)

    def weigh(values, weights):
        return lax.dot_general(
            values, weights, (((0,), (0,)), ((), ())), preferred_element_type=jnp.float32
        )

    scores = mm(keys_new, qt_ref[...])
    key_pos = lax.broadcasted_iota(jnp.int32, (rows, columns), 0)
    query_pos = lax.broadcasted_iota(jnp.int32, (rows, columns), 1) % rows
    scores = jnp.where(key_pos <= query_pos, scores, neg_large)
    top = jnp.max(scores, axis=0, keepdims=True)
    weights = jnp.exp(scores - top)
    top_ref[...] = top
    total_ref[...] = jnp.sum(weights, axis=0, keepdims=True)
    acc_ref[...] = weigh(values_new, weights.astype(jnp.bfloat16))

    def visit(block_idx, masked):
        start = pl.multiple_of(block_idx * key_block, key_block)
        scores = mm(kc_ref[0, pl.ds(start, key_block), :], qt_ref[...])
        if masked:
            place = start + lax.broadcasted_iota(jnp.int32, (key_block, columns), 0)
            first = length - WINDOW + 1 + lax.broadcasted_iota(jnp.int32, (1, columns), 1) % rows
            live = (place < length) & ((place < SINK) | (place >= first))
            scores = jnp.where(live, scores, neg_large)
        top_old = top_ref[...]
        top_new = jnp.maximum(top_old, jnp.max(scores, axis=0, keepdims=True))
        weights = jnp.exp(scores - top_new)
        factor = jnp.exp(top_old - top_new)
        top_ref[...] = top_new
        total_ref[...] = total_ref[...] * factor + jnp.sum(weights, axis=0, keepdims=True)
        acc_ref[...] = acc_ref[...] * factor + weigh(
            vc_ref[0, pl.ds(start, key_block), :], weights.astype(jnp.bfloat16)
        )

    blocks = (length + key_block - 1) // key_block
    low = jnp.minimum(
        (jnp.maximum(length + rows - WINDOW, 0) + key_block - 1) // key_block, blocks
    )
    high = jnp.maximum(low, length // key_block)

    def run(begin, end, masked):
        def step(block_idx, carried):
            visit(block_idx, masked)
            return carried

        lax.fori_loop(begin, end, step, 0)

    run(0, low, True)
    run(low, high, False)
    run(high, blocks, True)
    result = acc_ref[...] / total_ref[...]
    parts = []
    for h in range(heads):
        kv = h // share
        parts.append(result[kv * HD : (kv + 1) * HD, h * rows : (h + 1) * rows])
    heads_rows = jnp.concatenate(parts, axis=0).T.astype(jnp.bfloat16)
    out_ref[...] = mm(heads_rows, wo_ref[...]).astype(jnp.bfloat16)


def attend(past_len, tokens, gain, w_query, w_key, w_value, w_out, cache_keys, cache_values):
    requests, capacity, kv_width = cache_keys.shape
    group_rows, width = tokens.shape
    rows = group_rows // requests
    key_block = math.gcd(capacity, 512)
    columns = w_query.shape[1] // HD * rows

    def whole(array):
        return pl.BlockSpec(
            array.shape, lambda i, lens: (0,) * array.ndim, pipeline_mode=pl.Buffered(1)
        )

    gain = gain.reshape(1, width)
    cache_spec = pl.BlockSpec((1, capacity, kv_width), lambda i, lens: (i, 0, 0))
    row_spec = pl.BlockSpec((rows, width), lambda i, lens: (i, 0))
    return pl.pallas_call(
        functools.partial(attend_kernel, key_block),
        out_shape=jax.ShapeDtypeStruct((group_rows, width), jnp.bfloat16),
        grid_spec=pltpu.PrefetchScalarGridSpec(
            num_scalar_prefetch=1,
            grid=(requests,),
            in_specs=[row_spec]
            + [whole(a) for a in (gain, w_query, w_key, w_value, w_out)]
            + [cache_spec, cache_spec],
            out_specs=row_spec,
            scratch_shapes=[
                pltpu.VMEM((kv_width, columns), jnp.bfloat16),
                pltpu.VMEM((1, columns), jnp.float32),
                pltpu.VMEM((1, columns), jnp.float32),
                pltpu.VMEM((kv_width, columns), jnp.float32),
            ],
        ),
        compiler_params=pltpu.CompilerParams(vmem_limit_bytes=48 << 20),
        name="attend",
    )(past_len, tokens, gain, w_query, w_key, w_value, w_out, cache_keys, cache_values)


def start_if(cond, copy):
    pl.when(cond)(copy.start)


def greet(targets):
    barrier = pltpu.get_barrier_semaphore()
    total = 0
    for cond, device in targets:

        @pl.when(cond)
        def _():
            pl.semaphore_signal(
                barrier, inc=1, device_id=device, device_id_type=pl.DeviceIdType.MESH
            )

        total = total + jnp.where(cond, 1, 0)
    pl.semaphore_wait(barrier, total)


def send(src, dst, send_sem, recv_sem, device):
    return pltpu.make_async_remote_copy(
        src_ref=src,
        dst_ref=dst,
        send_sem=send_sem,
        recv_sem=recv_sem,
        device_id=device,
        device_id_type=pl.DeviceIdType.MESH,
    )


def moe_kernel(
    dp_size, chips, proj_ref, tok_ref, moe_gain_ref, final_gain_ref, router_ref, chosen_ref,
    win_hbm, wout_hbm,
    out_ref,
    mine_ref, got_ref, stream_ref, all_ref, win_ref, wout_ref, x_ref, sel_ref, gate_ref, rank_ref,
    gcol_ref, before_ref, part_ref, sib_ref, land_ref,
    tok_sem, rs_send, rs_recv, w_sem, z_send, z_recv, s_send, s_recv, p_send, p_recv, c_send, c_recv,
):
    rows, width = stream_ref.shape
    slots = win_ref.shape[0]
    cap = sel_ref.shape[1] // slots
    ff = wout_ref.shape[1]
    pair = 2 * rows
    hops = z_send.shape[2]
    parts = c_send.shape[1]
    hop_rows, part_rows = rows // hops, rows // parts
    dp, ex = lax.axis_index("dp"), lax.axis_index("expert")
    chip, core = ex // 2, ex % 2
    upper, lower = chip < chips - 1, chip > 0
    sibling = (dp, chip * 2 + 1 - core)
    above = jnp.minimum(chip + 1, chips - 1)
    below = jnp.maximum(chip - 1, 0)

    def toward(d):
        return (dp, jnp.where(d == 0, above, below) * 2 + core)

    load = pltpu.make_async_copy(tok_ref.at[pl.ds(dp * rows, rows)], mine_ref, tok_sem)
    load.start()

    def weights(s):
        return (
            pltpu.make_async_copy(win_hbm.at[s], win_ref.at[s], w_sem.at[s, 0]),
            pltpu.make_async_copy(wout_hbm.at[s], wout_ref.at[s], w_sem.at[s, 1]),
        )

    greet(
        [(chip >= 0, (lax.rem(dp + k, dp_size), ex)) for k in range(1, dp_size)]
        + [(chip >= 0, sibling), (upper, (dp, above * 2 + core)), (lower, (dp, below * 2 + core))]
    )
    copies = []
    for k in range(1, dp_size):
        peer = lax.rem(dp + k, dp_size)
        copy = send(
            proj_ref.at[pl.ds(peer * rows, rows)],
            got_ref.at[k - 1],
            rs_send.at[k - 1],
            rs_recv.at[k - 1],
            (peer, ex),
        )
        copy.start()
        copies.append(copy)

    @pl.loop(0, slots)
    def _(s):
        for copy in weights(s):
            copy.start()

    before_ref[...] = jnp.where(
        lax.broadcasted_iota(jnp.int32, (pair, pair), 0)
        < lax.broadcasted_iota(jnp.int32, (pair, pair), 1),
        1.0,
        0.0,
    ).astype(jnp.bfloat16)
    load.wait()
    attn = proj_ref[pl.ds(dp * rows, rows), :].astype(jnp.float32)
    for k, copy in enumerate(copies):
        copy.wait()
        attn = attn + got_ref[k].astype(jnp.float32)
    stream = mine_ref[...].astype(jnp.float32) + attn
    stream_ref[...] = stream
    all_ref[chip * 2 + core] = rms_scale(stream, moe_gain_ref[...]).astype(jnp.bfloat16)

    def along(d, origin, j):
        block = all_ref.at[origin * 2 + core, pl.ds(j * hop_rows, hop_rows)]
        return send(block, block, z_send.at[d, origin, j], z_recv.at[d, origin, j], toward(d))

    def across(origin, j, owner):
        block = all_ref.at[origin * 2 + owner, pl.ds(j * hop_rows, hop_rows)]
        return send(block, block, s_send.at[origin, j], s_recv.at[origin, j], sibling)

    def halves(origin):
        return send(
            part_ref.at[origin, 1 - core],
            sib_ref.at[origin],
            p_send.at[origin],
            p_recv.at[origin],
            sibling,
        )

    def onward(d, dest, k):
        here = pl.ds(k * part_rows, part_rows)
        arrives = jnp.where((d == 1) & (dest == below), chips, dest)
        return send(
            part_ref.at[dest, core, here],
            land_ref.at[arrives, here],
            c_send.at[dest, k],
            c_recv.at[arrives, k],
            toward(d),
        )

    def landed(place, k):
        here = pl.ds(k * part_rows, part_rows)
        return send(
            part_ref.at[0, core, here],
            land_ref.at[place, here],
            c_send.at[0, k],
            c_recv.at[place, k],
            sibling,
        )

    for j in range(hops):
        start_if(upper, along(0, chip, j))
        start_if(lower, along(1, chip, j))
        across(chip, j, core).start()

    def forward(step, j):
        for d in range(2):
            origin = chip - step if d == 0 else chip + step
            valid = (origin >= 0) & (origin < chips)
            bounded = jnp.clip(origin, 0, chips - 1)

            @pl.when(valid)
            def _():
                along(d, bounded, j).wait_recv()
                across(bounded, j, core).start()

            start_if(valid & (upper if d == 0 else lower), along(d, bounded, j))

    def side_of(step, side):
        origin = chip + (2 * side - 1) * step
        valid = (origin >= 0) & (origin < chips) & ((step > 0) | (side == 0))
        return jnp.clip(origin, 0, chips - 1), valid

    def take(origin, side):
        for j in range(hops):
            across(origin, j, 1 - core).wait_recv()
        block = all_ref[pl.ds(origin * 2, 2)].reshape(pair, width)
        logits = lax.dot_general(
            router_ref[...], block, (((1,), (1,)), ((), ())), preferred_element_type=jnp.float32
        )
        used = jnp.concatenate([chosen_ref[origin * 2], chosen_ref[origin * 2 + 1]], axis=1)
        chosen = used.astype(jnp.float32) > 0.0
        top = jnp.max(jnp.where(chosen, logits, neg_large), axis=0, keepdims=True)
        soft = jnp.where(chosen, jnp.exp(jnp.where(chosen, logits, top) - top), 0.0)
        gate_ref[...] = soft / jnp.sum(soft, axis=0, keepdims=True)
        rank_ref[...] = jnp.where(chosen, mm(used, before_ref[...]), -1.0)
        wanted = lax.broadcasted_iota(jnp.int32, (cap, pair), 0).astype(jnp.float32)
        for s in range(slots):
            row = pl.ds(ex * slots + s, 1)
            mine = wanted == rank_ref[row, :]
            sel_ref[side, s * cap : (s + 1) * cap, :] = jnp.where(mine, 1.0, 0.0).astype(jnp.bfloat16)
            gcol_ref[side, s * cap : (s + 1) * cap, :] = jnp.sum(
                jnp.where(mine, gate_ref[row, :], 0.0), axis=1, keepdims=True
            )
        for n in range(0, width, 256):
            columns = slice(n, n + 256)
            taken = mm(sel_ref[side], all_ref[pl.ds(origin * 2, 2), :, columns].reshape(pair, 256))
            x_ref[side, :, columns] = taken.astype(jnp.bfloat16)

    def give(origin, side):
        for n in range(0, width, 256):
            columns = slice(n, n + 256)
            spread = lax.dot_general(
                sel_ref[side],
                x_ref[side, :, columns],
                (((0,), (0,)), ((), ())),
                preferred_element_type=jnp.float32,
            )
            part_ref[origin, :, :, columns] = spread.reshape(2, rows, 256).astype(jnp.bfloat16)
        halves(origin).start()

    def combine(step):
        for side in range(2):
            origin, valid = side_of(step, side)

            @pl.when(valid)
            def _():
                halves(origin).wait_recv()
                total = part_ref[origin, core].astype(jnp.float32)
                total = total + sib_ref[origin].astype(jnp.float32)
                part_ref[origin, core] = total.astype(jnp.bfloat16)

            first = chip == 0 if side == 1 else chip == chips - 1

            @pl.when(valid & first & (step > 0))
            def _():
                for k in range(parts):
                    onward(1 - side, origin, k).start()

    @pl.loop(0, chips)
    def _(step):
        @pl.loop(0, 2)
        def _(side):
            origin, valid = side_of(step, side)
            pl.when(valid)(lambda: take(origin, side))

        pl.when(step > 0)(lambda: combine(step - 1))
        busy = side_of(step, 0)[1] | side_of(step, 1)[1]

        @pl.when(busy)
        def _():
            @pl.loop(0, slots)
            def _(s):
                @pl.when(step == 0)
                def _():
                    for copy in weights(s):
                        copy.wait()

                here = pl.ds(pl.multiple_of(s * cap, cap), cap)
                gate_up = mm(x_ref[:, here, :].reshape(2 * cap, width), win_ref[s])
                g = gate_up[:, :ff]
                activation = (g / (1.0 + jnp.exp(-g)) * gate_up[:, ff:]).astype(jnp.bfloat16)
                gate = gcol_ref[:, here, :].reshape(2 * cap, 1)
                produced = (mm(activation, wout_ref[s]) * gate).astype(jnp.bfloat16)
                x_ref[:, here, :] = produced.reshape(2, cap, width)
                for j in range(hops):
                    pl.when(s == (j + 1) * slots // hops - 1)(lambda: forward(step + 1, j))

            @pl.loop(0, 2)
            def _(side):
                origin, valid = side_of(step, side)
                pl.when(valid)(lambda: give(origin, side))

    combine(chips - 1)

    @pl.loop(1, chips)
    def _(key):
        @pl.loop(0, parts)
        def _(k):
            for which in range(2):
                d = jnp.where(chip < chips // 2, which, 1 - which)
                place = jnp.where(d == 0, chip, chips - 1 - chip)
                dest = jnp.where(d == 0, key, chips - 1 - key)
                arrives = jnp.where((d == 1) & (dest == chip), chips, dest)

                @pl.when((place > 0) & (key >= place))
                def _():
                    landed(arrives, k).wait_recv()

                @pl.when((place > 0) & (key > place))
                def _():
                    here = pl.ds(pl.multiple_of(k * part_rows, part_rows), part_rows)
                    total = part_ref[dest, core, here].astype(jnp.float32)
                    total = total + land_ref[dest, here].astype(jnp.float32)
                    part_ref[dest, core, here] = total.astype(jnp.bfloat16)
                    onward(d, dest, k).start()

    total = stream_ref[...] + part_ref[chip, core].astype(jnp.float32)
    total = total + jnp.where(lower, land_ref[chip].astype(jnp.float32), 0.0)
    total = total + jnp.where(upper, land_ref[chips].astype(jnp.float32), 0.0)
    out_ref[...] = rms_scale(total, final_gain_ref[...]).astype(jnp.bfloat16)

    @pl.loop(0, chips)
    def _(origin):
        for j in range(hops):
            pl.when(upper & (origin <= chip))(along(0, origin, j).wait_send)
            pl.when(lower & (origin >= chip))(along(1, origin, j).wait_send)
            across(origin, j, core).wait_send()
        halves(origin).wait_send()
        for k in range(parts):
            pl.when(origin > chip)(onward(0, origin, k).wait_send)
            pl.when(origin < chip)(onward(1, origin, k).wait_send)


def moe(projected, tokens, moe_gain, final_gain, router_t, chosen, expert_in, expert_out, dp_size, ex_size):
    group_rows, width = tokens.shape
    rows = group_rows // dp_size
    chips = ex_size // 2
    slots, _, double = expert_in.shape
    ff = expert_out.shape[1]
    cap = 2 * MOST
    hops, parts = 2, 4
    dma = pltpu.SemaphoreType.DMA
    vmem = pl.BlockSpec(memory_space=pltpu.VMEM)
    hbm = pl.BlockSpec(memory_space=pl.ANY)
    bf16, f32 = jnp.bfloat16, jnp.float32
    return pl.pallas_call(
        functools.partial(moe_kernel, dp_size, chips),
        out_shape=jax.ShapeDtypeStruct((rows, width), bf16),
        in_specs=[vmem, hbm] + [vmem] * 4 + [hbm] * 2,
        out_specs=vmem,
        scratch_shapes=[
            pltpu.VMEM((rows, width), bf16),
            pltpu.VMEM((dp_size - 1, rows, width), bf16),
            pltpu.VMEM((rows, width), f32),
            pltpu.VMEM((2 * chips, rows, width), bf16),
            pltpu.VMEM((slots, width, double), bf16),
            pltpu.VMEM((slots, ff, width), bf16),
            pltpu.VMEM((2, slots * cap, width), bf16),
            pltpu.VMEM((2, slots * cap, 2 * rows), bf16),
            pltpu.VMEM((chosen.shape[1], 2 * rows), f32),
            pltpu.VMEM((chosen.shape[1], 2 * rows), f32),
            pltpu.VMEM((2, slots * cap, 1), f32),
            pltpu.VMEM((2 * rows, 2 * rows), bf16),
            pltpu.VMEM((chips, 2, rows, width), bf16),
            pltpu.VMEM((chips, rows, width), bf16),
            pltpu.VMEM((chips + 1, rows, width), bf16),
            dma,
            dma((dp_size - 1,)),
            dma((dp_size - 1,)),
            dma((slots, 2)),
            dma((2, chips, hops)),
            dma((2, chips, hops)),
            dma((chips, hops)),
            dma((chips, hops)),
            dma((chips,)),
            dma((chips,)),
            dma((chips, parts)),
            dma((chips + 1, parts)),
        ],
        compiler_params=pltpu.CompilerParams(
            collective_id=0, has_side_effects=True, vmem_limit_bytes=62 << 20
        ),
        name="moe",
    )(
        projected,
        tokens,
        moe_gain.reshape(1, width),
        final_gain.reshape(1, width),
        router_t,
        chosen,
        expert_in,
        expert_out,
    )


def choose_slots(slot_owner, routes, split_pick):
    slot_ids = jnp.arange(slot_owner.shape[0], dtype=jnp.int32)
    same_owner = slot_owner[:, None] == slot_owner[None, :]
    slot_rank = jnp.sum(
        (same_owner & (slot_ids[None, :] < slot_ids[:, None])).astype(jnp.int32), axis=1
    )
    routes_t, pick_t = routes.T, split_pick.T
    serving = slot_owner[:, None, None] == routes_t[None, :, :]
    replicas = jnp.sum(serving.astype(jnp.int32), axis=0)
    wanted = pick_t % replicas
    hits = serving & (slot_rank[:, None, None] == wanted[None, :, :])
    return jnp.any(hits, axis=1).astype(jnp.bfloat16)


def shards(
    tokens,
    past_len,
    cache_keys,
    cache_values,
    attn_gain,
    w_query,
    w_key,
    w_value,
    w_out,
    moe_gain,
    router,
    expert_in,
    expert_out,
    final_gain,
    slot_owner,
    routes,
    split_pick,
):
    dp_size, ex_size = lax.axis_size("dp"), lax.axis_size("expert")
    chosen = choose_slots(slot_owner, routes, split_pick)
    chosen = lax.all_gather(chosen, "expert", axis=0)
    pick = slot_owner[:, None] == jnp.arange(router.shape[1], dtype=jnp.int32)[None, :]
    router_t = mm(pick.astype(jnp.bfloat16), router.T).astype(jnp.bfloat16)
    projected = attend(
        past_len, tokens, attn_gain, w_query, w_key, w_value, w_out, cache_keys, cache_values
    )
    return moe(
        projected, tokens, moe_gain, final_gain, router_t, chosen, expert_in, expert_out,
        dp_size, ex_size,
    )


def solution(mesh):
    return jax.shard_map(
        shards,
        mesh=mesh,
        in_specs=(
            P("expert", None),
            P("expert"),
            P("expert", None, "dp"),
            P("expert", None, "dp"),
            P(),
            P(None, "dp"),
            P(None, "dp"),
            P(None, "dp"),
            P("dp", None),
            P(),
            P(),
            P("expert", None, None),
            P("expert", None, None),
            P(),
            P(),
            P(("expert", "dp"), None),
            P(("expert", "dp"), None),
        ),
        out_specs=P(("expert", "dp"), None),
        check_vma=False,
    )
```

```python
import functools

import jax
import jax.numpy as jnp
from jax import lax
from jax.experimental import pallas as pl
from jax.experimental.pallas import tpu as pltpu
from jax.sharding import PartitionSpec as P

HD = 64
SINK = 4
WINDOW = 4096
MOST = 40
KEY_BLOCK = 512
GROUPS = 3

epsilon = 1e-05
neg_large = -1e30


def rms_scale(values, gain):
    widened = values.astype(jnp.float32)
    mean_square = jnp.mean(widened * widened, axis=-1, keepdims=True)
    return widened * lax.rsqrt(mean_square + epsilon) * gain


def mm(a, b):
    return jnp.dot(a, b, preferred_element_type=jnp.float32)


def start_if(cond, copy):
    pl.when(cond)(copy.start)


def send(src, dst, send_sem, recv_sem, device):
    return pltpu.make_async_remote_copy(
        src_ref=src,
        dst_ref=dst,
        send_sem=send_sem,
        recv_sem=recv_sem,
        device_id=device,
        device_id_type=pl.DeviceIdType.MESH,
    )


def layer_kernel(
    dp_size, ex_size, len_ref, owner_ref, routes_ref, pick_ref, attn_gain_ref, moe_gain_ref, final_gain_ref,
    router_ref, tok_hbm, wq_hbm, wk_hbm, wv_hbm, wo_hbm, kc_hbm, vc_hbm, win_hbm, wout_hbm,
    out_ref,
    qt_ref, top_ref, total_ref, acc_ref, score_ref, peak_ref,
    stream_ref, all_ref, win_ref, wout_ref, x_ref, sel_ref, gate_ref, rank_ref,
    gcol_ref, before_ref, part_ref, sib_ref, land_ref, chosen_ref, slot_router_ref,
    tok_sem, proj_sem, kv_sem, m_send, m_recv, rs_send, rs_recv, w_sem,
    z_send, z_recv, s_send, s_recv, p_send, p_recv, c_send, c_recv,
):
    chips = ex_size // 2
    rows, width = stream_ref.shape
    slots = win_ref.shape[0]
    all_slots = gate_ref.shape[0]
    cap = sel_ref.shape[1] // slots
    ff = wout_ref.shape[1]
    pair = 2 * rows
    hops = z_send.shape[2]
    parts = c_send.shape[1]
    hop_rows, part_rows = rows // hops, rows // parts
    dp, ex = lax.axis_index("dp"), lax.axis_index("expert")
    chip, core = ex // 2, ex % 2
    upper, lower = chip < chips - 1, chip > 0
    sibling = (dp, chip * 2 + 1 - core)
    above = jnp.minimum(chip + 1, chips - 1)
    below = jnp.maximum(chip - 1, 0)
    bf16, f32 = jnp.bfloat16, jnp.float32

    def toward(d):
        return (dp, jnp.where(d == 0, above, below) * 2 + core)

    def weights(s):
        return (
            pltpu.make_async_copy(win_hbm.at[s], win_ref.at[s], w_sem.at[s, 0]),
            pltpu.make_async_copy(wout_hbm.at[s], wout_ref.at[s], w_sem.at[s, 1]),
        )

    peers = [(lax.rem(dp + k, dp_size), ex) for k in range(1, dp_size)]
    peers += [(dp, lax.rem(ex + k, ex_size)) for k in range(1, ex_size)]
    barrier = pltpu.get_barrier_semaphore()
    for peer in peers:
        pl.semaphore_signal(barrier, inc=1, device_id=peer, device_id_type=pl.DeviceIdType.MESH)

    requests, capacity, kv_width = kc_hbm.shape
    q_width = wq_hbm.shape[1]
    heads, kv_local = q_width // HD, kv_width // HD
    share = heads // kv_local
    columns = heads * rows
    group = columns // GROUPS
    blocks = capacity // KEY_BLOCK
    stack = width // KEY_BLOCK
    ring = stack * (win_ref.shape[2] // (2 * kv_width))
    ahead = min(ring - 4, blocks)
    proj, pool = win_ref.at[slots - 1], win_ref.at[slots - 2]
    wq_ref = proj.at[:, 0:q_width]
    wk_ref = proj.at[:, q_width : q_width + kv_width]
    wv_ref = proj.at[:, q_width + kv_width : q_width + 2 * kv_width]
    wo_ref = wout_ref.at[slots - 1, 0:q_width]
    half = requests // 2

    def sent(r):
        return part_ref.at[r // 2, r % 2]

    def token(r):
        return part_ref.at[half + r // 2, r % 2]

    def token_copy(r):
        return pltpu.make_async_copy(tok_hbm.at[pl.ds(r * rows, rows)], token(r), tok_sem.at[r])

    proj_copies = [
        pltpu.make_async_copy(src, dst, proj_sem.at[n])
        for n, (src, dst) in enumerate(
            ((wq_hbm, wq_ref), (wk_hbm, wk_ref), (wv_hbm, wv_ref), (wo_hbm, wo_ref))
        )
    ]

    def request_at(step):
        return lax.rem(dp + 1 + step, dp_size)

    def spot(number, which):
        place = lax.rem(number, ring)
        row = pl.multiple_of(lax.rem(place, stack) * KEY_BLOCK, KEY_BLOCK)
        column = pl.multiple_of((place // stack) * 2 * kv_width + which * kv_width, kv_width)
        return pl.ds(row, KEY_BLOCK), pl.ds(column, kv_width)

    def kv_copies(number):
        r, i = request_at(number // blocks), lax.rem(number, blocks)
        here = pl.ds(pl.multiple_of(i * KEY_BLOCK, KEY_BLOCK), KEY_BLOCK)
        place = lax.rem(number, ring)
        return [
            pltpu.make_async_copy(src.at[r, here], pool.at[spot(number, n)], kv_sem.at[place, n])
            for n, src in enumerate((kc_hbm, vc_hbm))
        ]

    token_copy(request_at(0)).start()
    for copy in proj_copies:
        copy.start()

    @pl.loop(0, ahead)
    def _(number):
        for copy in kv_copies(number):
            copy.start()

    for step in range(1, dp_size):
        token_copy(request_at(step)).start()

    routes = routes_ref[...]
    lanes = lax.broadcasted_iota(jnp.int32, (1, rows), 1)

    replicas = jnp.zeros(routes.shape, f32)
    for s in range(all_slots):
        owner = owner_ref[s]
        rank_ref[s : s + 1, :rows] = jnp.where(lanes == owner, 1.0, 0.0)
        replicas = replicas + jnp.where(routes == owner, 1.0, 0.0)
    picks = pick_ref[...].astype(f32)
    turn = picks - jnp.floor((picks + 0.5) / replicas) * replicas

    seen = jnp.zeros(routes.shape, f32)
    for s in range(all_slots):
        serving = routes == owner_ref[s]
        hit = jnp.where(serving & (seen == turn), 1.0, 0.0)
        gate_ref[s : s + 1, :rows] = jnp.max(hit, axis=0, keepdims=True)
        seen = seen + jnp.where(serving, 1.0, 0.0)
    chosen_ref[ex] = gate_ref[:, :rows].astype(bf16)
    spots = router_ref.shape[0]
    slot_router_ref[...] = mm(rank_ref[:, :spots].astype(bf16), router_ref[...]).astype(bf16)
    before_ref[...] = jnp.where(
        lax.broadcasted_iota(jnp.int32, (pair, pair), 0)
        < lax.broadcasted_iota(jnp.int32, (pair, pair), 1),
        1.0,
        0.0,
    ).astype(bf16)
    qt_ref[:kv_width] = jnp.zeros((kv_width, columns), bf16)
    gap = lax.broadcasted_iota(jnp.int32, (rows, columns), 0)
    query = lax.broadcasted_iota(jnp.int32, (rows, columns), 1) % rows
    qt_ref[kv_width:] = jnp.where((query > gap) | (gap == rows - 1), neg_large, 0.0).astype(bf16)
    pl.semaphore_wait(barrier, len(peers))

    def masks(k):
        return send(
            chosen_ref.at[ex],
            chosen_ref.at[ex],
            m_send.at[k - 1],
            m_recv.at[k - 1],
            (dp, lax.rem(ex + k, ex_size)),
        )

    def masks_from(k):
        origin = lax.rem(ex + ex_size - k, ex_size)
        return send(
            chosen_ref.at[ex], chosen_ref.at[origin], m_send.at[k - 1], m_recv.at[k - 1], sibling
        )

    for k in range(1, ex_size):
        masks(k).start()

    def weigh(values, weights16):
        return lax.dot_general(
            values, weights16, (((0,), (0,)), ((), ())), preferred_element_type=f32
        )

    def share_out(step):
        return send(
            sent(request_at(step)),
            sib_ref.at[step],
            rs_send.at[step],
            rs_recv.at[step],
            (request_at(step), ex),
        )

    @pl.loop(0, dp_size)
    def _(step):
        r = request_at(step)
        length = len_ref[r]
        token_copy(r).wait()

        @pl.when(step == 0)
        def _():
            for copy in proj_copies:
                copy.wait()

        normed = rms_scale(token(r)[...], attn_gain_ref[...].reshape(1, width)).astype(bf16)
        queries = mm(normed, wq_ref[...]).astype(bf16).astype(f32) * HD ** (-0.5)
        queries_t = queries.T.astype(bf16)
        for h in range(heads):
            kv = h // share
            qt_ref[kv * HD : (kv + 1) * HD, h * rows : (h + 1) * rows] = queries_t[
                h * HD : (h + 1) * HD, :
            ]
        keys_new = mm(normed, wk_ref[...]).astype(bf16)
        values_new = mm(normed, wv_ref[...]).astype(bf16)
        scores = mm(keys_new, qt_ref[:kv_width])
        key_pos = lax.broadcasted_iota(jnp.int32, (rows, columns), 0)
        query_pos = lax.broadcasted_iota(jnp.int32, (rows, columns), 1) % rows
        scores = jnp.where(key_pos <= query_pos, scores, neg_large)
        top = jnp.max(scores, axis=0, keepdims=True)
        weights_new = jnp.exp(scores - top)
        top_ref[...] = top
        total_ref[...] = jnp.sum(weights_new, axis=0, keepdims=True)
        acc_ref[...] = weigh(values_new, weights_new.astype(bf16))

        def keys_of(i):
            keys = pool[spot(step * blocks + i, 0)]
            place = i * KEY_BLOCK + lax.broadcasted_iota(jnp.int32, (KEY_BLOCK, rows), 0)
            reach = place - (length - WINDOW + 1)
            past_sink = place >= SINK
            dead = (place >= length) | ((reach < 0) & past_sink)
            partial = past_sink & (reach < rows - 1)
            mark = jnp.where(dead, rows - 1, jnp.where(partial, reach, -1))
            lane = lax.broadcasted_iota(jnp.int32, (KEY_BLOCK, rows), 1)
            hot = jnp.where(mark == lane, 1.0, 0.0).astype(bf16)
            return jnp.concatenate([keys, hot], axis=1)

        def front(keys, buffer, g):
            c = slice(g * group, (g + 1) * group)
            scores = mm(keys, qt_ref[:, c])
            score_ref[buffer, :, c] = scores
            peak_ref[buffer, :, c] = jnp.max(scores, axis=0, keepdims=True)

        def back(i, buffer, g):
            c = slice(g * group, (g + 1) * group)
            values = pool[spot(step * blocks + i, 1)]
            top_old = top_ref[:, c]
            top_new = jnp.maximum(top_old, peak_ref[buffer, :, c])
            factor = jnp.exp(top_old - top_new)
            weights32 = jnp.exp(score_ref[buffer, :, c] - top_new)
            top_ref[:, c] = top_new
            total_ref[:, c] = total_ref[:, c] * factor + jnp.sum(weights32, axis=0, keepdims=True)
            acc_ref[:, c] = acc_ref[:, c] * factor + weigh(values, weights32.astype(bf16))

        def arrive(i):
            number = step * blocks + i

            @pl.when(number + ahead < dp_size * blocks)
            def _():
                for copy in kv_copies(number + ahead):
                    copy.start()

            for copy in kv_copies(number):
                copy.wait()

        arrive(0)
        keys = keys_of(0)
        for g in range(GROUPS):
            front(keys, 0, g)

        @pl.loop(0, (blocks - 1) // 2)
        def _(pair_id):
            for buffer in range(2):
                i = pair_id * 2 + buffer
                arrive(i + 1)
                keys = keys_of(i + 1)
                for g in range(GROUPS):
                    front(keys, 1 - buffer, g)
                    back(i, buffer, g)

        if blocks % 2 == 0:
            arrive(blocks - 1)
            keys = keys_of(blocks - 1)
            for g in range(GROUPS):
                front(keys, 1, g)
                back(blocks - 2, 0, g)
        for g in range(GROUPS):
            back(blocks - 1, (blocks - 1) % 2, g)
        result = acc_ref[...] / total_ref[...]
        pieces = []
        for h in range(heads):
            kv = h // share
            pieces.append(result[kv * HD : (kv + 1) * HD, h * rows : (h + 1) * rows])
        heads_rows = jnp.concatenate(pieces, axis=0).T.astype(bf16)
        sent(r)[...] = mm(heads_rows, wo_ref[...]).astype(bf16)
        pl.when(step < dp_size - 1)(lambda: share_out(step).start())

        @pl.when(step == 0)
        def _():
            @pl.loop(0, slots - 2)
            def _(s):
                for copy in weights(s):
                    copy.start()

    @pl.loop(slots - 2, slots)
    def _(s):
        for copy in weights(s):
            copy.start()

    attn = sent(dp)[...].astype(f32)
    for step in range(dp_size - 1):
        share_out(step).wait()
        attn = attn + sib_ref[step].astype(f32)
    stream = token(dp)[...].astype(f32) + attn
    stream_ref[...] = stream
    all_ref[chip * 2 + core] = rms_scale(stream, moe_gain_ref[...].reshape(1, width)).astype(bf16)

    def along(d, origin, j):
        block = all_ref.at[origin * 2 + core, pl.ds(j * hop_rows, hop_rows)]
        return send(block, block, z_send.at[d, origin, j], z_recv.at[d, origin, j], toward(d))

    def across(origin, j, owner):
        block = all_ref.at[origin * 2 + owner, pl.ds(j * hop_rows, hop_rows)]
        return send(block, block, s_send.at[origin, j], s_recv.at[origin, j], sibling)

    def halves(origin):
        return send(
            part_ref.at[origin, 1 - core],
            sib_ref.at[origin],
            p_send.at[origin],
            p_recv.at[origin],
            sibling,
        )

    def onward(d, dest, k):
        here = pl.ds(k * part_rows, part_rows)
        arrives = jnp.where((d == 1) & (dest == below), chips, dest)
        return send(
            part_ref.at[dest, core, here],
            land_ref.at[arrives, here],
            c_send.at[dest, k],
            c_recv.at[arrives, k],
            toward(d),
        )

    def landed(place, k):
        here = pl.ds(k * part_rows, part_rows)
        return send(
            part_ref.at[0, core, here],
            land_ref.at[place, here],
            c_send.at[0, k],
            c_recv.at[place, k],
            sibling,
        )

    for j in range(hops):
        start_if(upper, along(0, chip, j))
        start_if(lower, along(1, chip, j))
        across(chip, j, core).start()
    for k in range(1, ex_size):
        masks_from(k).wait_recv()
        masks(k).wait_send()

    def forward(step, j):
        for d in range(2):
            origin = chip - step if d == 0 else chip + step
            valid = (origin >= 0) & (origin < chips)
            bounded = jnp.clip(origin, 0, chips - 1)

            @pl.when(valid)
            def _():
                along(d, bounded, j).wait_recv()
                across(bounded, j, core).start()

            start_if(valid & (upper if d == 0 else lower), along(d, bounded, j))

    def side_of(step, side):
        origin = chip + (2 * side - 1) * step
        valid = (origin >= 0) & (origin < chips) & ((step > 0) | (side == 0))
        return jnp.clip(origin, 0, chips - 1), valid

    def take(origin, side):
        for j in range(hops):
            across(origin, j, 1 - core).wait_recv()
        block = all_ref[pl.ds(origin * 2, 2)].reshape(pair, width)
        logits = lax.dot_general(
            slot_router_ref[...], block, (((1,), (1,)), ((), ())), preferred_element_type=jnp.float32
        )
        used = jnp.concatenate([chosen_ref[origin * 2], chosen_ref[origin * 2 + 1]], axis=1)
        chosen = used.astype(jnp.float32) > 0.0
        top = jnp.max(jnp.where(chosen, logits, neg_large), axis=0, keepdims=True)
        soft = jnp.where(chosen, jnp.exp(jnp.where(chosen, logits, top) - top), 0.0)
        gate_ref[...] = soft / jnp.sum(soft, axis=0, keepdims=True)
        rank_ref[...] = jnp.where(chosen, mm(used, before_ref[...]), -1.0)
        wanted = lax.broadcasted_iota(jnp.int32, (cap, pair), 0).astype(jnp.float32)
        for s in range(slots):
            row = pl.ds(ex * slots + s, 1)
            mine = wanted == rank_ref[row, :]
            sel_ref[side, s * cap : (s + 1) * cap, :] = jnp.where(mine, 1.0, 0.0).astype(jnp.bfloat16)
            gcol_ref[side, s * cap : (s + 1) * cap, :] = jnp.sum(
                jnp.where(mine, gate_ref[row, :], 0.0), axis=1, keepdims=True
            )
        for n in range(0, width, 256):
            columns = slice(n, n + 256)
            taken = mm(sel_ref[side], all_ref[pl.ds(origin * 2, 2), :, columns].reshape(pair, 256))
            x_ref[side, :, columns] = taken.astype(jnp.bfloat16)

    def give(origin, side):
        for n in range(0, width, 256):
            columns = slice(n, n + 256)
            spread = lax.dot_general(
                sel_ref[side],
                x_ref[side, :, columns],
                (((0,), (0,)), ((), ())),
                preferred_element_type=jnp.float32,
            )
            part_ref[origin, :, :, columns] = spread.reshape(2, rows, 256).astype(jnp.bfloat16)
        halves(origin).start()

    def combine(step):
        for side in range(2):
            origin, valid = side_of(step, side)

            @pl.when(valid)
            def _():
                halves(origin).wait_recv()
                total = part_ref[origin, core].astype(jnp.float32)
                total = total + sib_ref[origin].astype(jnp.float32)
                part_ref[origin, core] = total.astype(jnp.bfloat16)

            first = chip == 0 if side == 1 else chip == chips - 1

            @pl.when(valid & first & (step > 0))
            def _():
                for k in range(parts):
                    onward(1 - side, origin, k).start()

    @pl.loop(0, chips)
    def _(step):
        @pl.loop(0, 2)
        def _(side):
            origin, valid = side_of(step, side)
            pl.when(valid)(lambda: take(origin, side))

        pl.when(step > 0)(lambda: combine(step - 1))
        busy = side_of(step, 0)[1] | side_of(step, 1)[1]

        @pl.when(busy)
        def _():
            @pl.loop(0, slots)
            def _(s):
                @pl.when(step == 0)
                def _():
                    for copy in weights(s):
                        copy.wait()

                here = pl.ds(pl.multiple_of(s * cap, cap), cap)
                gate_up = mm(x_ref[:, here, :].reshape(2 * cap, width), win_ref[s])
                g = gate_up[:, :ff]
                activation = (g / (1.0 + jnp.exp(-g)) * gate_up[:, ff:]).astype(jnp.bfloat16)
                gate = gcol_ref[:, here, :].reshape(2 * cap, 1)
                produced = (mm(activation, wout_ref[s]) * gate).astype(jnp.bfloat16)
                x_ref[:, here, :] = produced.reshape(2, cap, width)
                for j in range(hops):
                    pl.when(s == (j + 1) * slots // hops - 1)(lambda: forward(step + 1, j))

            @pl.loop(0, 2)
            def _(side):
                origin, valid = side_of(step, side)
                pl.when(valid)(lambda: give(origin, side))

    combine(chips - 1)

    @pl.loop(1, chips)
    def _(key):
        @pl.loop(0, parts)
        def _(k):
            for which in range(2):
                d = jnp.where(chip < chips // 2, which, 1 - which)
                place = jnp.where(d == 0, chip, chips - 1 - chip)
                dest = jnp.where(d == 0, key, chips - 1 - key)
                arrives = jnp.where((d == 1) & (dest == chip), chips, dest)

                @pl.when((place > 0) & (key >= place))
                def _():
                    landed(arrives, k).wait_recv()

                @pl.when((place > 0) & (key > place))
                def _():
                    here = pl.ds(pl.multiple_of(k * part_rows, part_rows), part_rows)
                    total = part_ref[dest, core, here].astype(jnp.float32)
                    total = total + land_ref[dest, here].astype(jnp.float32)
                    part_ref[dest, core, here] = total.astype(jnp.bfloat16)
                    onward(d, dest, k).start()

    total = stream_ref[...] + part_ref[chip, core].astype(jnp.float32)
    total = total + jnp.where(lower, land_ref[chip].astype(jnp.float32), 0.0)
    total = total + jnp.where(upper, land_ref[chips].astype(jnp.float32), 0.0)
    out_ref[...] = rms_scale(total, final_gain_ref[...].reshape(1, width)).astype(jnp.bfloat16)

    @pl.loop(0, chips)
    def _(origin):
        for j in range(hops):
            pl.when(upper & (origin <= chip))(along(0, origin, j).wait_send)
            pl.when(lower & (origin >= chip))(along(1, origin, j).wait_send)
            across(origin, j, core).wait_send()
        halves(origin).wait_send()
        for k in range(parts):
            pl.when(origin > chip)(onward(0, origin, k).wait_send)
            pl.when(origin < chip)(onward(1, origin, k).wait_send)


def layer(
    past_len, slot_owner, routes_t, pick_t, attn_gain, moe_gain, final_gain, router_t,
    tokens, w_query, w_key, w_value, w_out, cache_keys, cache_values, expert_in, expert_out,
    all_slots, dp_size, ex_size,
):
    group_rows, width = tokens.shape
    rows = group_rows // dp_size
    requests, capacity, kv_width = cache_keys.shape
    assert requests == dp_size and rows == 128 and capacity % KEY_BLOCK == 0
    chips = ex_size // 2
    slots, _, double = expert_in.shape
    ff = expert_out.shape[1]
    columns = w_query.shape[1] // HD * rows
    cap = 2 * MOST
    hops, parts = 2, 4
    ring = (width // KEY_BLOCK) * (double // (2 * kv_width))
    dma = pltpu.SemaphoreType.DMA
    vmem = pl.BlockSpec(memory_space=pltpu.VMEM)
    smem = pl.BlockSpec(memory_space=pltpu.SMEM)
    hbm = pl.BlockSpec(memory_space=pl.ANY)
    bf16, f32 = jnp.bfloat16, jnp.float32
    return pl.pallas_call(
        functools.partial(layer_kernel, dp_size, ex_size),
        out_shape=jax.ShapeDtypeStruct((rows, width), bf16),
        in_specs=[smem] * 2 + [vmem] * 6 + [hbm] * 9,
        out_specs=vmem,
        scratch_shapes=[
            pltpu.VMEM((2 * kv_width, columns), bf16),
            pltpu.VMEM((1, columns), f32),
            pltpu.VMEM((1, columns), f32),
            pltpu.VMEM((kv_width, columns), f32),
            pltpu.VMEM((2, KEY_BLOCK, columns), f32),
            pltpu.VMEM((2, 1, columns), f32),
            pltpu.VMEM((rows, width), f32),
            pltpu.VMEM((2 * chips, rows, width), bf16),
            pltpu.VMEM((slots, width, double), bf16),
            pltpu.VMEM((slots, ff, width), bf16),
            pltpu.VMEM((2, slots * cap, width), bf16),
            pltpu.VMEM((2, slots * cap, 2 * rows), bf16),
            pltpu.VMEM((all_slots, 2 * rows), f32),
            pltpu.VMEM((all_slots, 2 * rows), f32),
            pltpu.VMEM((2, slots * cap, 1), f32),
            pltpu.VMEM((2 * rows, 2 * rows), bf16),
            pltpu.VMEM((max(chips, requests), 2, rows, width), bf16),
            pltpu.VMEM((max(chips, dp_size - 1), rows, width), bf16),
            pltpu.VMEM((chips + 1, rows, width), bf16),
            pltpu.VMEM((ex_size, all_slots, rows), bf16),
            pltpu.VMEM((all_slots, width), bf16),
            dma((requests,)),
            dma((4,)),
            dma((ring, 2)),
            dma((ex_size - 1,)),
            dma((ex_size - 1,)),
            dma((dp_size - 1,)),
            dma((dp_size - 1,)),
            dma((slots, 2)),
            dma((2, chips, hops)),
            dma((2, chips, hops)),
            dma((chips, hops)),
            dma((chips, hops)),
            dma((chips,)),
            dma((chips,)),
            dma((chips, parts)),
            dma((chips + 1, parts)),
        ],
        compiler_params=pltpu.CompilerParams(
            collective_id=0, has_side_effects=True, vmem_limit_bytes=63 << 20
        ),
        name="layer",
    )(
        past_len, slot_owner, routes_t, pick_t, attn_gain, moe_gain, final_gain, router_t,
        tokens, w_query, w_key, w_value, w_out, cache_keys, cache_values, expert_in, expert_out,
    )


def shards(
    tokens,
    past_len,
    cache_keys,
    cache_values,
    attn_gain,
    w_query,
    w_key,
    w_value,
    w_out,
    moe_gain,
    router,
    expert_in,
    expert_out,
    final_gain,
    slot_owner,
    routes,
    split_pick,
):
    return layer(
        past_len, slot_owner, routes.T, split_pick.T, attn_gain, moe_gain, final_gain, router.T,
        tokens, w_query, w_key, w_value, w_out, cache_keys, cache_values, expert_in, expert_out,
        slot_owner.shape[0], lax.axis_size("dp"), lax.axis_size("expert"),
    )


def solution(mesh):
    return jax.shard_map(
        shards,
        mesh=mesh,
        in_specs=(
            P("expert", None),
            P("expert"),
            P("expert", None, "dp"),
            P("expert", None, "dp"),
            P(),
            P(None, "dp"),
            P(None, "dp"),
            P(None, "dp"),
            P("dp", None),
            P(),
            P(),
            P("expert", None, None),
            P("expert", None, None),
            P(),
            P(),
            P(("expert", "dp"), None),
            P(("expert", "dp"), None),
        ),
        out_specs=P(("expert", "dp"), None),
        check_vma=False,
    )
```

```python
import functools

import jax
import jax.numpy as jnp
from jax import lax
from jax.experimental import pallas as pl
from jax.experimental.pallas import tpu as pltpu
from jax.sharding import PartitionSpec as P

HD = 64
SINK = 4
WINDOW = 4096
MOST = 40
KEY_BLOCK = 512
GROUPS = 3
LAG = 4

epsilon = 1e-05
neg_large = -1e30


def rms_scale(values, gain):
    widened = values.astype(jnp.float32)
    mean_square = jnp.mean(widened * widened, axis=-1, keepdims=True)
    return widened * lax.rsqrt(mean_square + epsilon) * gain


def mm(a, b):
    return jnp.dot(a, b, preferred_element_type=jnp.float32)


def start_if(cond, copy):
    pl.when(cond)(copy.start)


def send(src, dst, send_sem, recv_sem, device):
    return pltpu.make_async_remote_copy(
        src_ref=src,
        dst_ref=dst,
        send_sem=send_sem,
        recv_sem=recv_sem,
        device_id=device,
        device_id_type=pl.DeviceIdType.MESH,
    )


def layer_kernel(
    dp_size, ex_size, len_ref, owner_ref, routes_ref, pick_ref, attn_gain_ref, moe_gain_ref, final_gain_ref,
    router_ref, tok_hbm, wq_hbm, wk_hbm, wv_hbm, wo_hbm, kc_hbm, vc_hbm, win_hbm, wout_hbm,
    out_ref,
    qt_ref, top_ref, total_ref, acc_ref, score_ref, peak_ref,
    stream_ref, all_ref, win_ref, wout_ref, x_ref, sel_ref, gate_ref, rank_ref,
    gcol_ref, before_ref, part_ref, sib_ref, land_ref, chosen_ref, slot_router_ref,
    tok_sem, proj_sem, kv_sem, m_send, m_recv, rs_send, rs_recv, w_sem,
    z_send, z_recv, s_send, s_recv, p_send, p_recv, c_send, c_recv,
):
    chips = ex_size // 2
    rows, width = stream_ref.shape
    slots = win_ref.shape[0]
    all_slots = gate_ref.shape[0]
    cap = sel_ref.shape[1] // slots
    ff = wout_ref.shape[1]
    pair = 2 * rows
    hops = z_send.shape[2]
    parts = c_send.shape[1]
    hop_rows, part_rows = rows // hops, rows // parts
    dp, ex = lax.axis_index("dp"), lax.axis_index("expert")
    chip, core = ex // 2, ex % 2
    upper, lower = chip < chips - 1, chip > 0
    sibling = (dp, chip * 2 + 1 - core)
    above = jnp.minimum(chip + 1, chips - 1)
    below = jnp.maximum(chip - 1, 0)
    bf16, f32 = jnp.bfloat16, jnp.float32

    def toward(d):
        return (dp, jnp.where(d == 0, above, below) * 2 + core)

    def weights(s):
        return (
            pltpu.make_async_copy(win_hbm.at[s], win_ref.at[s], w_sem.at[s, 0]),
            pltpu.make_async_copy(wout_hbm.at[s], wout_ref.at[s], w_sem.at[s, 1]),
        )

    peers = [(lax.rem(dp + k, dp_size), ex) for k in range(1, dp_size)]
    peers += [(dp, lax.rem(ex + k, ex_size)) for k in range(1, ex_size)]
    barrier = pltpu.get_barrier_semaphore()
    for peer in peers:
        pl.semaphore_signal(barrier, inc=1, device_id=peer, device_id_type=pl.DeviceIdType.MESH)

    requests, capacity, kv_width = kc_hbm.shape
    q_width = wq_hbm.shape[1]
    heads, kv_local = q_width // HD, kv_width // HD
    share = heads // kv_local
    columns = heads * rows
    group = columns // GROUPS
    blocks = capacity // KEY_BLOCK
    stack = width // KEY_BLOCK
    ring = stack * (win_ref.shape[2] // (2 * kv_width))
    ahead = min(ring - 4, blocks)
    proj, pool = win_ref.at[slots - 1], win_ref.at[slots - 2]
    wq_ref = proj.at[:, 0:q_width]
    wk_ref = proj.at[:, q_width : q_width + kv_width]
    wv_ref = proj.at[:, q_width + kv_width : q_width + 2 * kv_width]
    wo_ref = wout_ref.at[slots - 1, 0:q_width]
    half = requests // 2

    def sent(r):
        return part_ref.at[r // 2, r % 2]

    def token(r):
        return part_ref.at[half + r // 2, r % 2]

    def token_copy(r):
        return pltpu.make_async_copy(tok_hbm.at[pl.ds(r * rows, rows)], token(r), tok_sem.at[r])

    proj_copies = [
        pltpu.make_async_copy(src, dst, proj_sem.at[n])
        for n, (src, dst) in enumerate(
            ((wq_hbm, wq_ref), (wk_hbm, wk_ref), (wv_hbm, wv_ref), (wo_hbm, wo_ref))
        )
    ]

    def request_at(step):
        return lax.rem(dp + 1 + step, dp_size)

    def spot(number, which):
        place = lax.rem(number, ring)
        row = pl.multiple_of(lax.rem(place, stack) * KEY_BLOCK, KEY_BLOCK)
        column = pl.multiple_of((place // stack) * 2 * kv_width + which * kv_width, kv_width)
        return pl.ds(row, KEY_BLOCK), pl.ds(column, kv_width)

    def kv_copies(number):
        r, i = request_at(number // blocks), lax.rem(number, blocks)
        here = pl.ds(pl.multiple_of(i * KEY_BLOCK, KEY_BLOCK), KEY_BLOCK)
        place = lax.rem(number, ring)
        return [
            pltpu.make_async_copy(src.at[r, here], pool.at[spot(number, n)], kv_sem.at[place, n])
            for n, src in enumerate((kc_hbm, vc_hbm))
        ]

    token_copy(request_at(0)).start()
    for copy in proj_copies:
        copy.start()

    @pl.loop(0, ahead)
    def _(number):
        for copy in kv_copies(number):
            copy.start()

    for step in range(1, dp_size):
        token_copy(request_at(step)).start()

    routes = routes_ref[...]
    lanes = lax.broadcasted_iota(jnp.int32, (1, rows), 1)

    replicas = jnp.zeros(routes.shape, f32)
    for s in range(all_slots):
        owner = owner_ref[s]
        rank_ref[s : s + 1, :rows] = jnp.where(lanes == owner, 1.0, 0.0)
        replicas = replicas + jnp.where(routes == owner, 1.0, 0.0)
    picks = pick_ref[...].astype(f32)
    turn = picks - jnp.floor((picks + 0.5) / replicas) * replicas

    seen = jnp.zeros(routes.shape, f32)
    for s in range(all_slots):
        serving = routes == owner_ref[s]
        hit = jnp.where(serving & (seen == turn), 1.0, 0.0)
        gate_ref[s : s + 1, :rows] = jnp.max(hit, axis=0, keepdims=True)
        seen = seen + jnp.where(serving, 1.0, 0.0)
    chosen_ref[ex] = gate_ref[:, :rows].astype(bf16)
    spots = router_ref.shape[0]
    slot_router_ref[...] = mm(rank_ref[:, :spots].astype(bf16), router_ref[...]).astype(bf16)
    before_ref[...] = jnp.where(
        lax.broadcasted_iota(jnp.int32, (pair, pair), 0)
        < lax.broadcasted_iota(jnp.int32, (pair, pair), 1),
        1.0,
        0.0,
    ).astype(bf16)
    qt_ref[:kv_width] = jnp.zeros((kv_width, columns), bf16)
    gap = lax.broadcasted_iota(jnp.int32, (rows, columns), 0)
    query = lax.broadcasted_iota(jnp.int32, (rows, columns), 1) % rows
    qt_ref[kv_width:] = jnp.where((query > gap) | (gap == rows - 1), neg_large, 0.0).astype(bf16)
    pl.semaphore_wait(barrier, len(peers))

    def masks(k):
        return send(
            chosen_ref.at[ex],
            chosen_ref.at[ex],
            m_send.at[k - 1],
            m_recv.at[k - 1],
            (dp, lax.rem(ex + k, ex_size)),
        )

    def masks_from(k):
        origin = lax.rem(ex + ex_size - k, ex_size)
        return send(
            chosen_ref.at[ex], chosen_ref.at[origin], m_send.at[k - 1], m_recv.at[k - 1], sibling
        )

    for k in range(1, ex_size):
        masks(k).start()

    def weigh(values, weights16):
        return lax.dot_general(
            values, weights16, (((0,), (0,)), ((), ())), preferred_element_type=f32
        )

    def share_out(step):
        return send(
            sent(request_at(step)),
            sib_ref.at[step],
            rs_send.at[step],
            rs_recv.at[step],
            (request_at(step), ex),
        )

    def arrive(number):
        @pl.when(number + ahead < dp_size * blocks)
        def _():
            for copy in kv_copies(number + ahead):
                copy.start()

        for copy in kv_copies(number):
            copy.wait()

    for copy in proj_copies:
        copy.wait()
    for r in range(requests):
        token_copy(r).wait()
    group_tokens = part_ref[half : 2 * half].reshape(requests * rows, width)
    normed = rms_scale(group_tokens, attn_gain_ref[...].reshape(1, width)).astype(bf16)
    queries = mm(normed, wq_ref[...]).astype(bf16) * jnp.asarray(HD ** (-0.5), bf16)
    keys_all = mm(normed, wk_ref[...]).astype(bf16)
    values_all = mm(normed, wv_ref[...]).astype(bf16)
    for r in range(requests):
        here = slice(r * rows, (r + 1) * rows)
        x_ref[0, :rows, r * q_width : (r + 1) * q_width] = queries[here]
        x_ref[1, :rows, 2 * r * kv_width : (2 * r + 1) * kv_width] = keys_all[here]
        x_ref[1, :rows, (2 * r + 1) * kv_width : (2 * r + 2) * kv_width] = values_all[here]

    @pl.loop(0, dp_size)
    def _(step):
        r = request_at(step)
        length = len_ref[r]
        arrive(step * blocks)
        queries_t = x_ref[0, :rows, pl.ds(pl.multiple_of(r * q_width, q_width), q_width)].T
        for h in range(heads):
            kv = h // share
            qt_ref[kv * HD : (kv + 1) * HD, h * rows : (h + 1) * rows] = queries_t[
                h * HD : (h + 1) * HD, :
            ]
        fresh = pl.multiple_of(r * 2 * kv_width, 2 * kv_width)
        keys_new = x_ref[1, :rows, pl.ds(fresh, kv_width)]
        values_new = x_ref[1, :rows, pl.ds(pl.multiple_of(fresh + kv_width, kv_width), kv_width)]
        scores = mm(keys_new, qt_ref[:kv_width])
        key_pos = lax.broadcasted_iota(jnp.int32, (rows, columns), 0)
        query_pos = lax.broadcasted_iota(jnp.int32, (rows, columns), 1) % rows
        scores = jnp.where(key_pos <= query_pos, scores, neg_large)
        top = jnp.max(scores, axis=0, keepdims=True)
        weights_new = jnp.exp(scores - top)
        top_ref[...] = top
        total_ref[...] = jnp.sum(weights_new, axis=0, keepdims=True)
        acc_ref[...] = weigh(values_new, weights_new.astype(bf16))

        def keys_of(i):
            keys = pool[spot(step * blocks + i, 0)]
            start = i * KEY_BLOCK
            slot_id = lax.broadcasted_iota(jnp.int32, (KEY_BLOCK, rows), 0)
            reach = slot_id + (start - (length - WINDOW + 1))
            mark = jnp.where(slot_id >= length - start, -1, jnp.maximum(reach, -1))
            mark = jnp.where(slot_id < jnp.minimum(length, SINK) - start, rows, mark)
            lane = lax.broadcasted_iota(jnp.int32, (KEY_BLOCK, rows), 1)
            lane = jnp.where(lane == rows - 1, -1, lane)
            hot = jnp.where(mark == lane, 1.0, 0.0).astype(bf16)
            return jnp.concatenate([keys, hot], axis=1)

        def front(keys, buffer, g):
            c = slice(g * group, (g + 1) * group)
            scores = mm(keys, qt_ref[:, c])
            score_ref[buffer, :, c] = scores
            peak_ref[buffer, :, c] = jnp.max(scores, axis=0, keepdims=True)

        def back(i, buffer, g):
            c = slice(g * group, (g + 1) * group)
            values = pool[spot(step * blocks + i, 1)]
            top_old = top_ref[:, c]
            top_new = jnp.maximum(top_old, peak_ref[buffer, :, c])
            factor = jnp.exp(top_old - top_new)
            weights32 = jnp.exp(score_ref[buffer, :, c] - top_new)
            top_ref[:, c] = top_new
            total_ref[:, c] = total_ref[:, c] * factor + jnp.sum(weights32, axis=0, keepdims=True)
            acc_ref[:, c] = acc_ref[:, c] * factor + weigh(values, weights32.astype(bf16))

        keys = keys_of(0)
        for g in range(GROUPS):
            front(keys, 0, g)

        @pl.loop(0, (blocks - 1) // 2)
        def _(pair_id):
            for buffer in range(2):
                i = pair_id * 2 + buffer
                arrive(step * blocks + i + 1)
                keys = keys_of(i + 1)
                for g in range(GROUPS):
                    front(keys, 1 - buffer, g)
                    back(i, buffer, g)

        if blocks % 2 == 0:
            arrive(step * blocks + blocks - 1)
            keys = keys_of(blocks - 1)
            for g in range(GROUPS):
                front(keys, 1, g)
                back(blocks - 2, 0, g)
        for g in range(GROUPS):
            back(blocks - 1, (blocks - 1) % 2, g)
        result = acc_ref[...] / total_ref[...]
        pieces = []
        for h in range(heads):
            kv = h // share
            pieces.append(result[kv * HD : (kv + 1) * HD, h * rows : (h + 1) * rows])
        heads_rows = jnp.concatenate(pieces, axis=0).T.astype(bf16)
        sent(r)[...] = mm(heads_rows, wo_ref[...]).astype(bf16)
        pl.when(step < dp_size - 1)(lambda: share_out(step).start())

        @pl.when(step == 0)
        def _():
            @pl.loop(0, slots - 2)
            def _(s):
                for copy in weights(s):
                    copy.start()

    @pl.loop(slots - 2, slots)
    def _(s):
        for copy in weights(s):
            copy.start()

    attn = sent(dp)[...].astype(f32)
    for step in range(dp_size - 1):
        share_out(step).wait()
        attn = attn + sib_ref[step].astype(f32)
    stream = token(dp)[...].astype(f32) + attn
    stream_ref[...] = stream
    all_ref[chip * 2 + core] = rms_scale(stream, moe_gain_ref[...].reshape(1, width)).astype(bf16)

    def along(d, origin, j):
        block = all_ref.at[origin * 2 + core, pl.ds(j * hop_rows, hop_rows)]
        return send(block, block, z_send.at[d, origin, j], z_recv.at[d, origin, j], toward(d))

    def across(origin, j, owner):
        block = all_ref.at[origin * 2 + owner, pl.ds(j * hop_rows, hop_rows)]
        return send(block, block, s_send.at[origin, j], s_recv.at[origin, j], sibling)

    def halves(origin):
        return send(
            part_ref.at[origin, 1 - core],
            sib_ref.at[origin],
            p_send.at[origin],
            p_recv.at[origin],
            sibling,
        )

    def onward(d, dest, k):
        here = pl.ds(k * part_rows, part_rows)
        arrives = jnp.where((d == 1) & (dest == below), chips, dest)
        return send(
            part_ref.at[dest, core, here],
            land_ref.at[arrives, here],
            c_send.at[dest, k],
            c_recv.at[arrives, k],
            toward(d),
        )

    def landed(place, k):
        here = pl.ds(k * part_rows, part_rows)
        return send(
            part_ref.at[0, core, here],
            land_ref.at[place, here],
            c_send.at[0, k],
            c_recv.at[place, k],
            sibling,
        )

    for j in range(hops):
        start_if(upper, along(0, chip, j))
        start_if(lower, along(1, chip, j))
        across(chip, j, core).start()
    for k in range(1, ex_size):
        masks_from(k).wait_recv()
        masks(k).wait_send()

    def forward(step, j):
        for d in range(2):
            origin = chip - step if d == 0 else chip + step
            valid = (origin >= 0) & (origin < chips)
            bounded = jnp.clip(origin, 0, chips - 1)

            @pl.when(valid)
            def _():
                along(d, bounded, j).wait_recv()
                across(bounded, j, core).start()

            start_if(valid & (upper if d == 0 else lower), along(d, bounded, j))

    def side_of(step, side):
        origin = chip + (2 * side - 1) * step
        valid = (origin >= 0) & (origin < chips) & ((step > 0) | (side == 0))
        return jnp.clip(origin, 0, chips - 1), valid

    def take(origin, side):
        for j in range(hops):
            across(origin, j, 1 - core).wait_recv()
        block = all_ref[pl.ds(origin * 2, 2)].reshape(pair, width)
        logits = lax.dot_general(
            slot_router_ref[...], block, (((1,), (1,)), ((), ())), preferred_element_type=jnp.float32
        )
        used = jnp.concatenate([chosen_ref[origin * 2], chosen_ref[origin * 2 + 1]], axis=1)
        chosen = used.astype(jnp.float32) > 0.0
        top = jnp.max(jnp.where(chosen, logits, neg_large), axis=0, keepdims=True)
        soft = jnp.where(chosen, jnp.exp(jnp.where(chosen, logits, top) - top), 0.0)
        gate_ref[...] = soft / jnp.sum(soft, axis=0, keepdims=True)
        rank_ref[...] = jnp.where(chosen, mm(used, before_ref[...]), -1.0)
        wanted = lax.broadcasted_iota(jnp.int32, (cap, pair), 0).astype(jnp.float32)
        for s in range(slots):
            row = pl.ds(ex * slots + s, 1)
            mine = wanted == rank_ref[row, :]
            sel_ref[side, s * cap : (s + 1) * cap, :] = jnp.where(mine, 1.0, 0.0).astype(jnp.bfloat16)
            gcol_ref[side, s * cap : (s + 1) * cap, :] = jnp.sum(
                jnp.where(mine, gate_ref[row, :], 0.0), axis=1, keepdims=True
            )
        for n in range(0, width, 256):
            columns = slice(n, n + 256)
            taken = mm(sel_ref[side], all_ref[pl.ds(origin * 2, 2), :, columns].reshape(pair, 256))
            x_ref[side, :, columns] = taken.astype(jnp.bfloat16)

    def give(origin, side):
        for n in range(0, width, 256):
            columns = slice(n, n + 256)
            spread = lax.dot_general(
                sel_ref[side],
                x_ref[side, :, columns],
                (((0,), (0,)), ((), ())),
                preferred_element_type=jnp.float32,
            )
            part_ref[origin, :, :, columns] = spread.reshape(2, rows, 256).astype(jnp.bfloat16)
        halves(origin).start()

    def combine(step):
        for side in range(2):
            origin, valid = side_of(step, side)

            @pl.when(valid)
            def _():
                halves(origin).wait_recv()
                total = part_ref[origin, core].astype(jnp.float32)
                total = total + sib_ref[origin].astype(jnp.float32)
                part_ref[origin, core] = total.astype(jnp.bfloat16)

            first = chip == 0 if side == 1 else chip == chips - 1

            @pl.when(valid & first & (step > 0))
            def _():
                for k in range(parts):
                    onward(1 - side, origin, k).start()

    def expert(s):
        here = pl.ds(pl.multiple_of(s * cap, cap), cap)
        moe_in = x_ref[:, here, :].reshape(2 * cap, width)
        pieces = []
        for n in range(0, ff, 256):
            g = mm(moe_in, win_ref[s, :, n : n + 256])
            u = mm(moe_in, win_ref[s, :, ff + n : ff + n + 256])
            pieces.append((g / (1.0 + jnp.exp(-g)) * u).astype(bf16))
        activation = jnp.concatenate(pieces, axis=1)
        gate = gcol_ref[:, here, :].reshape(2 * cap, 1)
        for n in range(0, width, 256):
            produced = mm(activation, wout_ref[s, :, n : n + 256]) * gate
            x_ref[:, here, n : n + 256] = produced.astype(bf16).reshape(2, cap, 256)

    @pl.loop(0, chips)
    def _(step):
        @pl.loop(0, 2)
        def _(side):
            origin, valid = side_of(step, side)
            pl.when(valid)(lambda: take(origin, side))

        pl.when(step > 0)(lambda: combine(step - 1))
        busy = side_of(step, 0)[1] | side_of(step, 1)[1]

        @pl.when(busy)
        def _():
            @pl.loop(0, slots // 2)
            def _(couple):
                for s in (couple * 2, couple * 2 + 1):

                    @pl.when(step == 0)
                    def _():
                        for copy in weights(s):
                            copy.wait()

                for s in (couple * 2, couple * 2 + 1):
                    expert(s)
                for j in range(hops):
                    turn = (j + 1) * slots // (2 * hops) - 1
                    pl.when(couple == max(turn, 0))(lambda: forward(step + 1, j))

            @pl.loop(0, 2)
            def _(side):
                origin, valid = side_of(step, side)
                pl.when(valid)(lambda: give(origin, side))

    combine(chips - 1)

    turns = (chips - 1) * parts

    @pl.loop(0, turns + LAG)
    def _(turn):
        for which in range(2):
            number = turn - which * LAG
            key, k = 1 + number // parts, lax.rem(number, parts)
            d = jnp.where(chip < chips // 2, which, 1 - which)
            place = jnp.where(d == 0, chip, chips - 1 - chip)
            dest = jnp.where(d == 0, key, chips - 1 - key)

            @pl.when((number >= 0) & (number < turns) & (place > 0) & (key > place))
            def _():
                landed(dest, k).wait_recv()
                here = pl.ds(pl.multiple_of(k * part_rows, part_rows), part_rows)
                total = part_ref[dest, core, here].astype(jnp.float32)
                total = total + land_ref[dest, here].astype(jnp.float32)
                part_ref[dest, core, here] = total.astype(jnp.bfloat16)
                onward(d, dest, k).start()

    for k in range(parts):
        pl.when(lower)(landed(chip, k).wait_recv)
        pl.when(upper)(landed(chips, k).wait_recv)
    total = stream_ref[...] + part_ref[chip, core].astype(jnp.float32)
    total = total + jnp.where(lower, land_ref[chip].astype(jnp.float32), 0.0)
    total = total + jnp.where(upper, land_ref[chips].astype(jnp.float32), 0.0)
    out_ref[...] = rms_scale(total, final_gain_ref[...].reshape(1, width)).astype(jnp.bfloat16)

    @pl.loop(0, chips)
    def _(origin):
        for j in range(hops):
            pl.when(upper & (origin <= chip))(along(0, origin, j).wait_send)
            pl.when(lower & (origin >= chip))(along(1, origin, j).wait_send)
            across(origin, j, core).wait_send()
        halves(origin).wait_send()
        for k in range(parts):
            pl.when(origin > chip)(onward(0, origin, k).wait_send)
            pl.when(origin < chip)(onward(1, origin, k).wait_send)


def layer(
    past_len, slot_owner, routes_t, pick_t, attn_gain, moe_gain, final_gain, router_t,
    tokens, w_query, w_key, w_value, w_out, cache_keys, cache_values, expert_in, expert_out,
    all_slots, dp_size, ex_size,
):
    group_rows, width = tokens.shape
    rows = group_rows // dp_size
    requests, capacity, kv_width = cache_keys.shape
    assert requests == dp_size and rows == 128 and capacity % KEY_BLOCK == 0
    chips = ex_size // 2
    slots, _, double = expert_in.shape
    ff = expert_out.shape[1]
    columns = w_query.shape[1] // HD * rows
    cap = 2 * MOST
    hops, parts = 2, 8
    ring = (width // KEY_BLOCK) * (double // (2 * kv_width))
    dma = pltpu.SemaphoreType.DMA
    vmem = pl.BlockSpec(memory_space=pltpu.VMEM)
    smem = pl.BlockSpec(memory_space=pltpu.SMEM)
    hbm = pl.BlockSpec(memory_space=pl.ANY)
    bf16, f32 = jnp.bfloat16, jnp.float32
    return pl.pallas_call(
        functools.partial(layer_kernel, dp_size, ex_size),
        out_shape=jax.ShapeDtypeStruct((rows, width), bf16),
        in_specs=[smem] * 2 + [vmem] * 6 + [hbm] * 9,
        out_specs=vmem,
        scratch_shapes=[
            pltpu.VMEM((2 * kv_width, columns), bf16),
            pltpu.VMEM((1, columns), f32),
            pltpu.VMEM((1, columns), f32),
            pltpu.VMEM((kv_width, columns), f32),
            pltpu.VMEM((2, KEY_BLOCK, columns), f32),
            pltpu.VMEM((2, 1, columns), f32),
            pltpu.VMEM((rows, width), f32),
            pltpu.VMEM((2 * chips, rows, width), bf16),
            pltpu.VMEM((slots, width, double), bf16),
            pltpu.VMEM((slots, ff, width), bf16),
            pltpu.VMEM((2, slots * cap, width), bf16),
            pltpu.VMEM((2, slots * cap, 2 * rows), bf16),
            pltpu.VMEM((all_slots, 2 * rows), f32),
            pltpu.VMEM((all_slots, 2 * rows), f32),
            pltpu.VMEM((2, slots * cap, 1), f32),
            pltpu.VMEM((2 * rows, 2 * rows), bf16),
            pltpu.VMEM((max(chips, requests), 2, rows, width), bf16),
            pltpu.VMEM((max(chips, dp_size - 1), rows, width), bf16),
            pltpu.VMEM((chips + 1, rows, width), bf16),
            pltpu.VMEM((ex_size, all_slots, rows), bf16),
            pltpu.VMEM((all_slots, width), bf16),
            dma((requests,)),
            dma((4,)),
            dma((ring, 2)),
            dma((ex_size - 1,)),
            dma((ex_size - 1,)),
            dma((dp_size - 1,)),
            dma((dp_size - 1,)),
            dma((slots, 2)),
            dma((2, chips, hops)),
            dma((2, chips, hops)),
            dma((chips, hops)),
            dma((chips, hops)),
            dma((chips,)),
            dma((chips,)),
            dma((chips, parts)),
            dma((chips + 1, parts)),
        ],
        compiler_params=pltpu.CompilerParams(
            collective_id=0, has_side_effects=True, vmem_limit_bytes=63 << 20
        ),
        name="layer",
    )(
        past_len, slot_owner, routes_t, pick_t, attn_gain, moe_gain, final_gain, router_t,
        tokens, w_query, w_key, w_value, w_out, cache_keys, cache_values, expert_in, expert_out,
    )


def shards(
    tokens,
    past_len,
    cache_keys,
    cache_values,
    attn_gain,
    w_query,
    w_key,
    w_value,
    w_out,
    moe_gain,
    router,
    expert_in,
    expert_out,
    final_gain,
    slot_owner,
    routes,
    split_pick,
):
    return layer(
        past_len, slot_owner, routes.T, split_pick.T, attn_gain, moe_gain, final_gain, router.T,
        tokens, w_query, w_key, w_value, w_out, cache_keys, cache_values, expert_in, expert_out,
        slot_owner.shape[0], lax.axis_size("dp"), lax.axis_size("expert"),
    )


def solution(mesh):
    return jax.shard_map(
        shards,
        mesh=mesh,
        in_specs=(
            P("expert", None),
            P("expert"),
            P("expert", None, "dp"),
            P("expert", None, "dp"),
            P(),
            P(None, "dp"),
            P(None, "dp"),
            P(None, "dp"),
            P("dp", None),
            P(),
            P(),
            P("expert", None, None),
            P("expert", None, None),
            P(),
            P(),
            P(("expert", "dp"), None),
            P(("expert", "dp"), None),
        ),
        out_specs=P(("expert", "dp"), None),
        check_vma=False,
    )
```

```python
import functools

import jax
import jax.numpy as jnp
from jax import lax
from jax.experimental import pallas as pl
from jax.experimental.pallas import tpu as pltpu
from jax.sharding import PartitionSpec as P

HD = 64
SINK = 4
WINDOW = 4096
MOST = 40
KEY_BLOCK = 512
GROUPS = 3
LAG = 2

epsilon = 1e-05
neg_large = -1e30


def rms_scale(values, gain):
    widened = values.astype(jnp.float32)
    mean_square = jnp.mean(widened * widened, axis=-1, keepdims=True)
    return widened * lax.rsqrt(mean_square + epsilon) * gain


def mm(a, b):
    return jnp.dot(a, b, preferred_element_type=jnp.float32)


def start_if(cond, copy):
    pl.when(cond)(copy.start)


def send(src, dst, send_sem, recv_sem, device):
    return pltpu.make_async_remote_copy(
        src_ref=src,
        dst_ref=dst,
        send_sem=send_sem,
        recv_sem=recv_sem,
        device_id=device,
        device_id_type=pl.DeviceIdType.MESH,
    )


def layer_kernel(
    dp_size, ex_size, len_ref, owner_ref, routes_ref, pick_ref, attn_gain_ref, moe_gain_ref, final_gain_ref,
    router_ref, tok_hbm, wq_hbm, wk_hbm, wv_hbm, wo_hbm, kc_hbm, vc_hbm, win_hbm, wout_hbm,
    out_ref,
    qt_ref, top_ref, total_ref, acc_ref, score_ref, peak_ref,
    stream_ref, all_ref, win_ref, wout_ref, x_ref, sel_ref, gate_ref, rank_ref,
    gcol_ref, back_ref, before_ref, part_ref, sib_ref, land_ref, chosen_ref, slot_router_ref,
    tok_sem, proj_sem, kv_sem, m_send, m_recv, rs_send, rs_recv, w_sem,
    z_send, z_recv, s_send, s_recv, p_send, p_recv, c_send, c_recv,
):
    chips = ex_size // 2
    rows, width = stream_ref.shape
    slots = win_ref.shape[0]
    all_slots = gate_ref.shape[0]
    cap = sel_ref.shape[1] // slots
    ff = wout_ref.shape[1]
    pair = 2 * rows
    hops = z_send.shape[2]
    parts = c_send.shape[1]
    hop_rows, part_rows = rows // hops, rows // parts
    dp, ex = lax.axis_index("dp"), lax.axis_index("expert")
    chip, core = ex // 2, ex % 2
    upper, lower = chip < chips - 1, chip > 0
    sibling = (dp, chip * 2 + 1 - core)
    above = jnp.minimum(chip + 1, chips - 1)
    below = jnp.maximum(chip - 1, 0)
    bf16, f32 = jnp.bfloat16, jnp.float32

    def toward(d):
        return (dp, jnp.where(d == 0, above, below) * 2 + core)

    def weights(s):
        return (
            pltpu.make_async_copy(win_hbm.at[s], win_ref.at[s], w_sem.at[s, 0]),
            pltpu.make_async_copy(wout_hbm.at[s], wout_ref.at[s], w_sem.at[s, 1]),
        )

    peers = [(lax.rem(dp + k, dp_size), ex) for k in range(1, dp_size)]
    peers += [(dp, lax.rem(ex + k, ex_size)) for k in range(1, ex_size)]
    barrier = pltpu.get_barrier_semaphore()
    for peer in peers:
        pl.semaphore_signal(barrier, inc=1, device_id=peer, device_id_type=pl.DeviceIdType.MESH)

    requests, capacity, kv_width = kc_hbm.shape
    q_width = wq_hbm.shape[1]
    heads, kv_local = q_width // HD, kv_width // HD
    share = heads // kv_local
    columns = heads * rows
    group = columns // GROUPS
    blocks = capacity // KEY_BLOCK
    stack = width // KEY_BLOCK
    ring = stack * (win_ref.shape[2] // (2 * kv_width))
    ahead = min(ring - 4, blocks)
    proj, pool = win_ref.at[slots - 1], win_ref.at[slots - 2]
    wq_ref = proj.at[:, 0:q_width]
    wk_ref = proj.at[:, q_width : q_width + kv_width]
    wv_ref = proj.at[:, q_width + kv_width : q_width + 2 * kv_width]
    wo_ref = wout_ref.at[slots - 1, 0:q_width]
    half = requests // 2

    def sent(r):
        return part_ref.at[r // 2, r % 2]

    def token(r):
        return part_ref.at[half + r // 2, r % 2]

    def token_copy(r):
        return pltpu.make_async_copy(tok_hbm.at[pl.ds(r * rows, rows)], token(r), tok_sem.at[r])

    proj_copies = [
        pltpu.make_async_copy(src, dst, proj_sem.at[n])
        for n, (src, dst) in enumerate(
            ((wq_hbm, wq_ref), (wk_hbm, wk_ref), (wv_hbm, wv_ref), (wo_hbm, wo_ref))
        )
    ]

    def request_at(step):
        return lax.rem(dp + 1 + step, dp_size)

    def spot(number, which):
        place = lax.rem(number, ring)
        row = pl.multiple_of(lax.rem(place, stack) * KEY_BLOCK, KEY_BLOCK)
        column = pl.multiple_of((place // stack) * 2 * kv_width + which * kv_width, kv_width)
        return pl.ds(row, KEY_BLOCK), pl.ds(column, kv_width)

    def kv_copies(number):
        r, i = request_at(number // blocks), lax.rem(number, blocks)
        here = pl.ds(pl.multiple_of(i * KEY_BLOCK, KEY_BLOCK), KEY_BLOCK)
        place = lax.rem(number, ring)
        return [
            pltpu.make_async_copy(src.at[r, here], pool.at[spot(number, n)], kv_sem.at[place, n])
            for n, src in enumerate((kc_hbm, vc_hbm))
        ]

    token_copy(request_at(0)).start()
    for copy in proj_copies:
        copy.start()

    @pl.loop(0, ahead)
    def _(number):
        for copy in kv_copies(number):
            copy.start()

    for step in range(1, dp_size):
        token_copy(request_at(step)).start()

    routes = routes_ref[...]
    lanes = lax.broadcasted_iota(jnp.int32, (1, rows), 1)

    replicas = jnp.zeros(routes.shape, f32)
    for s in range(all_slots):
        owner = owner_ref[s]
        rank_ref[s : s + 1, :rows] = jnp.where(lanes == owner, 1.0, 0.0)
        replicas = replicas + jnp.where(routes == owner, 1.0, 0.0)
    picks = pick_ref[...].astype(f32)
    turn = picks - jnp.floor((picks + 0.5) / replicas) * replicas

    seen = jnp.zeros(routes.shape, f32)
    for s in range(all_slots):
        serving = routes == owner_ref[s]
        hit = jnp.where(serving & (seen == turn), 1.0, 0.0)
        gate_ref[s : s + 1, :rows] = jnp.max(hit, axis=0, keepdims=True)
        seen = seen + jnp.where(serving, 1.0, 0.0)
    chosen_ref[ex] = gate_ref[:, :rows].astype(bf16)
    spots = router_ref.shape[0]
    slot_router_ref[...] = mm(rank_ref[:, :spots].astype(bf16), router_ref[...]).astype(bf16)
    before_ref[...] = jnp.where(
        lax.broadcasted_iota(jnp.int32, (pair, pair), 0)
        < lax.broadcasted_iota(jnp.int32, (pair, pair), 1),
        1.0,
        0.0,
    ).astype(bf16)
    qt_ref[:kv_width] = jnp.zeros((kv_width, columns), bf16)
    gap = lax.broadcasted_iota(jnp.int32, (rows, columns), 0)
    query = lax.broadcasted_iota(jnp.int32, (rows, columns), 1) % rows
    qt_ref[kv_width:] = jnp.where((query > gap) | (gap == rows - 1), neg_large, 0.0).astype(bf16)
    pl.semaphore_wait(barrier, len(peers))

    def masks(k):
        return send(
            chosen_ref.at[ex],
            chosen_ref.at[ex],
            m_send.at[k - 1],
            m_recv.at[k - 1],
            (dp, lax.rem(ex + k, ex_size)),
        )

    def masks_from(k):
        origin = lax.rem(ex + ex_size - k, ex_size)
        return send(
            chosen_ref.at[ex], chosen_ref.at[origin], m_send.at[k - 1], m_recv.at[k - 1], sibling
        )

    for k in range(1, ex_size):
        masks(k).start()

    def weigh(values, weights16):
        return lax.dot_general(
            values, weights16, (((0,), (0,)), ((), ())), preferred_element_type=f32
        )

    def share_out(step):
        return send(
            sent(request_at(step)),
            sib_ref.at[step],
            rs_send.at[step],
            rs_recv.at[step],
            (request_at(step), ex),
        )

    def arrive(number):
        @pl.when(number + ahead < dp_size * blocks)
        def _():
            for copy in kv_copies(number + ahead):
                copy.start()

        for copy in kv_copies(number):
            copy.wait()

    for copy in proj_copies:
        copy.wait()
    for r in range(requests):
        token_copy(r).wait()
    group_tokens = part_ref[half : 2 * half].reshape(requests * rows, width)
    normed = rms_scale(group_tokens, attn_gain_ref[...].reshape(1, width)).astype(bf16)
    queries = mm(normed, wq_ref[...]).astype(bf16) * jnp.asarray(HD ** (-0.5), bf16)
    keys_all = mm(normed, wk_ref[...]).astype(bf16)
    values_all = mm(normed, wv_ref[...]).astype(bf16)
    for r in range(requests):
        here = slice(r * rows, (r + 1) * rows)
        x_ref[0, :rows, r * q_width : (r + 1) * q_width] = queries[here]
        x_ref[1, :rows, 2 * r * kv_width : (2 * r + 1) * kv_width] = keys_all[here]
        x_ref[1, :rows, (2 * r + 1) * kv_width : (2 * r + 2) * kv_width] = values_all[here]

    @pl.loop(0, dp_size)
    def _(step):
        r = request_at(step)
        length = len_ref[r]
        arrive(step * blocks)
        queries_t = x_ref[0, :rows, pl.ds(pl.multiple_of(r * q_width, q_width), q_width)].T
        for h in range(heads):
            kv = h // share
            qt_ref[kv * HD : (kv + 1) * HD, h * rows : (h + 1) * rows] = queries_t[
                h * HD : (h + 1) * HD, :
            ]
        fresh = pl.multiple_of(r * 2 * kv_width, 2 * kv_width)
        keys_new = x_ref[1, :rows, pl.ds(fresh, kv_width)]
        values_new = x_ref[1, :rows, pl.ds(pl.multiple_of(fresh + kv_width, kv_width), kv_width)]
        scores = mm(keys_new, qt_ref[:kv_width])
        key_pos = lax.broadcasted_iota(jnp.int32, (rows, columns), 0)
        query_pos = lax.broadcasted_iota(jnp.int32, (rows, columns), 1) % rows
        scores = jnp.where(key_pos <= query_pos, scores, neg_large)
        top = jnp.max(scores, axis=0, keepdims=True)
        weights_new = jnp.exp(scores - top)
        top_ref[...] = top
        total_ref[...] = jnp.sum(weights_new, axis=0, keepdims=True)
        acc_ref[...] = weigh(values_new, weights_new.astype(bf16))

        def keys_of(i):
            keys = pool[spot(step * blocks + i, 0)]
            start = i * KEY_BLOCK
            slot_id = lax.broadcasted_iota(jnp.int32, (KEY_BLOCK, rows), 0)
            reach = slot_id + (start - (length - WINDOW + 1))
            mark = jnp.where(slot_id >= length - start, -1, jnp.maximum(reach, -1))
            mark = jnp.where(slot_id < jnp.minimum(length, SINK) - start, rows, mark)
            lane = lax.broadcasted_iota(jnp.int32, (KEY_BLOCK, rows), 1)
            lane = jnp.where(lane == rows - 1, -1, lane)
            hot = jnp.where(mark == lane, 1.0, 0.0).astype(bf16)
            return jnp.concatenate([keys, hot], axis=1)

        def front(keys, buffer, g):
            c = slice(g * group, (g + 1) * group)
            scores = mm(keys, qt_ref[:, c])
            score_ref[buffer, :, c] = scores
            peak_ref[buffer, :, c] = jnp.max(scores, axis=0, keepdims=True)

        def back(i, buffer, g):
            c = slice(g * group, (g + 1) * group)
            values = pool[spot(step * blocks + i, 1)]
            top_old = top_ref[:, c]
            top_new = jnp.maximum(top_old, peak_ref[buffer, :, c])
            factor = jnp.exp(top_old - top_new)
            weights32 = jnp.exp(score_ref[buffer, :, c] - top_new)
            top_ref[:, c] = top_new
            total_ref[:, c] = total_ref[:, c] * factor + jnp.sum(weights32, axis=0, keepdims=True)
            acc_ref[:, c] = acc_ref[:, c] * factor + weigh(values, weights32.astype(bf16))

        keys = keys_of(0)
        for g in range(GROUPS):
            front(keys, 0, g)

        @pl.loop(0, (blocks - 1) // 2)
        def _(pair_id):
            for buffer in range(2):
                i = pair_id * 2 + buffer
                arrive(step * blocks + i + 1)
                keys = keys_of(i + 1)
                for g in range(GROUPS):
                    front(keys, 1 - buffer, g)
                    back(i, buffer, g)

        if blocks % 2 == 0:
            arrive(step * blocks + blocks - 1)
            keys = keys_of(blocks - 1)
            for g in range(GROUPS):
                front(keys, 1, g)
                back(blocks - 2, 0, g)
        for g in range(GROUPS):
            back(blocks - 1, (blocks - 1) % 2, g)
        result = acc_ref[...] / total_ref[...]
        pieces = []
        for h in range(heads):
            kv = h // share
            pieces.append(result[kv * HD : (kv + 1) * HD, h * rows : (h + 1) * rows])
        heads_rows = jnp.concatenate(pieces, axis=0).T.astype(bf16)
        sent(r)[...] = mm(heads_rows, wo_ref[...]).astype(bf16)
        pl.when(step < dp_size - 1)(lambda: share_out(step).start())

        share_of = -(-(slots - 2) // (dp_size - 1))

        @pl.when(step < dp_size - 1)
        def _():
            @pl.loop(step * share_of, jnp.minimum((step + 1) * share_of, slots - 2))
            def _(s):
                for copy in weights(s):
                    copy.start()

    attn = sent(dp)[...].astype(f32)
    for step in range(dp_size - 1):
        share_out(step).wait()
        attn = attn + sib_ref[step].astype(f32)
    stream = token(dp)[...].astype(f32) + attn
    stream_ref[...] = stream
    all_ref[chip * 2 + core] = rms_scale(stream, moe_gain_ref[...].reshape(1, width)).astype(bf16)

    def along(d, origin, j):
        block = all_ref.at[origin * 2 + core, pl.ds(j * hop_rows, hop_rows)]
        return send(block, block, z_send.at[d, origin, j], z_recv.at[d, origin, j], toward(d))

    def across(origin, j, owner):
        block = all_ref.at[origin * 2 + owner, pl.ds(j * hop_rows, hop_rows)]
        return send(block, block, s_send.at[origin, j], s_recv.at[origin, j], sibling)

    def halves(origin):
        return send(
            part_ref.at[origin, 1 - core],
            sib_ref.at[origin],
            p_send.at[origin],
            p_recv.at[origin],
            sibling,
        )

    def onward(d, dest, k):
        here = pl.ds(k * part_rows, part_rows)
        arrives = jnp.where((d == 1) & (dest == below), chips, dest)
        return send(
            part_ref.at[dest, core, here],
            land_ref.at[arrives, here],
            c_send.at[dest, k],
            c_recv.at[arrives, k],
            toward(d),
        )

    def landed(place, k):
        here = pl.ds(k * part_rows, part_rows)
        return send(
            part_ref.at[0, core, here],
            land_ref.at[place, here],
            c_send.at[0, k],
            c_recv.at[place, k],
            sibling,
        )

    for j in range(hops):
        start_if(upper, along(0, chip, j))
        start_if(lower, along(1, chip, j))
        across(chip, j, core).start()
    @pl.loop(slots - 2, slots)
    def _(s):
        for copy in weights(s):
            copy.start()

    for k in range(1, ex_size):
        masks_from(k).wait_recv()
        masks(k).wait_send()

    def forward(step, j):
        for d in range(2):
            origin = chip - step if d == 0 else chip + step
            valid = (origin >= 0) & (origin < chips)
            bounded = jnp.clip(origin, 0, chips - 1)

            @pl.when(valid)
            def _():
                along(d, bounded, j).wait_recv()
                across(bounded, j, core).start()

            start_if(valid & (upper if d == 0 else lower), along(d, bounded, j))

    def side_of(step, side):
        origin = chip + (2 * side - 1) * step
        valid = (origin >= 0) & (origin < chips) & ((step > 0) | (side == 0))
        return jnp.clip(origin, 0, chips - 1), valid

    def take(origin, side):
        for j in range(hops):
            across(origin, j, 1 - core).wait_recv()
        block = all_ref[pl.ds(origin * 2, 2)].reshape(pair, width)
        logits = lax.dot_general(
            slot_router_ref[...], block, (((1,), (1,)), ((), ())), preferred_element_type=jnp.float32
        )
        used = jnp.concatenate([chosen_ref[origin * 2], chosen_ref[origin * 2 + 1]], axis=1)
        chosen = used.astype(jnp.float32) > 0.0
        top = jnp.max(jnp.where(chosen, logits, neg_large), axis=0, keepdims=True)
        soft = jnp.where(chosen, jnp.exp(jnp.where(chosen, logits, top) - top), 0.0)
        gate_ref[...] = soft / jnp.sum(soft, axis=0, keepdims=True)
        rank_ref[...] = jnp.where(chosen, mm(used, before_ref[...]), -1.0)
        wanted = lax.broadcasted_iota(jnp.int32, (cap, pair), 0).astype(jnp.float32)
        for s in range(slots):
            row = pl.ds(ex * slots + s, 1)
            mine = wanted == rank_ref[row, :]
            sel_ref[side, s * cap : (s + 1) * cap, :] = jnp.where(mine, 1.0, 0.0).astype(jnp.bfloat16)
            gcol_ref[side, s * cap : (s + 1) * cap, :] = jnp.sum(
                jnp.where(mine, gate_ref[row, :], 0.0), axis=1, keepdims=True
            )
        back_ref[side] = sel_ref[side].T
        for n in range(0, width, 256):
            columns = slice(n, n + 256)
            taken = mm(sel_ref[side], all_ref[pl.ds(origin * 2, 2), :, columns].reshape(pair, 256))
            x_ref[side, :, columns] = taken.astype(jnp.bfloat16)

    def give(origin, side):
        for n in range(0, width, 256):
            columns = slice(n, n + 256)
            spread = mm(back_ref[side], x_ref[side, :, columns])
            part_ref[origin, :, :, columns] = spread.reshape(2, rows, 256).astype(jnp.bfloat16)
        halves(origin).start()

    def combine(step):
        for side in range(2):
            origin, valid = side_of(step, side)

            @pl.when(valid)
            def _():
                halves(origin).wait_recv()
                total = part_ref[origin, core].astype(jnp.float32)
                total = total + sib_ref[origin].astype(jnp.float32)
                part_ref[origin, core] = total.astype(jnp.bfloat16)

            first = chip == 0 if side == 1 else chip == chips - 1

            @pl.when(valid & first & (step > 0))
            def _():
                for k in range(parts):
                    onward(1 - side, origin, k).start()

    def expert(s):
        here = pl.ds(pl.multiple_of(s * cap, cap), cap)
        moe_in = x_ref[:, here, :].reshape(2 * cap, width)
        pieces = []
        for n in range(0, ff, 256):
            g = mm(moe_in, win_ref[s, :, n : n + 256])
            u = mm(moe_in, win_ref[s, :, ff + n : ff + n + 256])
            pieces.append((g / (1.0 + jnp.exp(-g)) * u).astype(bf16))
        activation = jnp.concatenate(pieces, axis=1)
        gate = gcol_ref[:, here, :].reshape(2 * cap, 1)
        for n in range(0, width, 256):
            produced = mm(activation, wout_ref[s, :, n : n + 256]) * gate
            x_ref[:, here, n : n + 256] = produced.astype(bf16).reshape(2, cap, 256)

    @pl.loop(0, chips)
    def _(step):
        @pl.loop(0, 2)
        def _(side):
            origin, valid = side_of(step, side)
            pl.when(valid)(lambda: take(origin, side))

        pl.when(step > 0)(lambda: combine(step - 1))
        busy = side_of(step, 0)[1] | side_of(step, 1)[1]

        @pl.when(busy)
        def _():
            @pl.loop(0, slots // 2)
            def _(couple):
                for s in (couple * 2, couple * 2 + 1):

                    @pl.when(step == 0)
                    def _():
                        for copy in weights(s):
                            copy.wait()

                for s in (couple * 2, couple * 2 + 1):
                    expert(s)
                first = jnp.where(step == 0, (slots // 2 - 1) // 2, 0)
                last = jnp.where(step == 0, slots // 2 - 1, max(slots // 2 - 2, 0))
                pl.when(couple == first)(lambda: forward(step + 1, 0))
                pl.when(couple == last)(lambda: forward(step + 1, 1))

            @pl.loop(0, 2)
            def _(side):
                origin, valid = side_of(step, side)
                pl.when(valid)(lambda: give(origin, side))

    combine(chips - 1)

    turns = (chips - 1) * parts

    @pl.loop(0, turns + LAG)
    def _(turn):
        for which in range(2):
            number = turn - which * LAG
            key, k = 1 + number // parts, lax.rem(number, parts)
            d = jnp.where(chip < chips // 2, which, 1 - which)
            place = jnp.where(d == 0, chip, chips - 1 - chip)
            dest = jnp.where(d == 0, key, chips - 1 - key)

            @pl.when((number >= 0) & (number < turns) & (place > 0) & (key > place))
            def _():
                landed(dest, k).wait_recv()
                here = pl.ds(pl.multiple_of(k * part_rows, part_rows), part_rows)
                total = part_ref[dest, core, here].astype(jnp.float32)
                total = total + land_ref[dest, here].astype(jnp.float32)
                part_ref[dest, core, here] = total.astype(jnp.bfloat16)
                onward(d, dest, k).start()

    for k in range(parts):
        pl.when(lower)(landed(chip, k).wait_recv)
        pl.when(upper)(landed(chips, k).wait_recv)
    total = stream_ref[...] + part_ref[chip, core].astype(jnp.float32)
    total = total + jnp.where(lower, land_ref[chip].astype(jnp.float32), 0.0)
    total = total + jnp.where(upper, land_ref[chips].astype(jnp.float32), 0.0)
    out_ref[...] = rms_scale(total, final_gain_ref[...].reshape(1, width)).astype(jnp.bfloat16)

    @pl.loop(0, chips)
    def _(origin):
        for j in range(hops):
            pl.when(upper & (origin <= chip))(along(0, origin, j).wait_send)
            pl.when(lower & (origin >= chip))(along(1, origin, j).wait_send)
            across(origin, j, core).wait_send()
        halves(origin).wait_send()
        for k in range(parts):
            pl.when(origin > chip)(onward(0, origin, k).wait_send)
            pl.when(origin < chip)(onward(1, origin, k).wait_send)


def layer(
    past_len, slot_owner, routes_t, pick_t, attn_gain, moe_gain, final_gain, router_t,
    tokens, w_query, w_key, w_value, w_out, cache_keys, cache_values, expert_in, expert_out,
    all_slots, dp_size, ex_size,
):
    group_rows, width = tokens.shape
    rows = group_rows // dp_size
    requests, capacity, kv_width = cache_keys.shape
    assert requests == dp_size and rows == 128 and capacity % KEY_BLOCK == 0
    chips = ex_size // 2
    slots, _, double = expert_in.shape
    ff = expert_out.shape[1]
    columns = w_query.shape[1] // HD * rows
    cap = 2 * MOST
    hops, parts = 2, 8
    ring = (width // KEY_BLOCK) * (double // (2 * kv_width))
    dma = pltpu.SemaphoreType.DMA
    vmem = pl.BlockSpec(memory_space=pltpu.VMEM)
    smem = pl.BlockSpec(memory_space=pltpu.SMEM)
    hbm = pl.BlockSpec(memory_space=pl.ANY)
    bf16, f32 = jnp.bfloat16, jnp.float32
    return pl.pallas_call(
        functools.partial(layer_kernel, dp_size, ex_size),
        out_shape=jax.ShapeDtypeStruct((rows, width), bf16),
        in_specs=[smem] * 2 + [vmem] * 6 + [hbm] * 9,
        out_specs=vmem,
        scratch_shapes=[
            pltpu.VMEM((2 * kv_width, columns), bf16),
            pltpu.VMEM((1, columns), f32),
            pltpu.VMEM((1, columns), f32),
            pltpu.VMEM((kv_width, columns), f32),
            pltpu.VMEM((2, KEY_BLOCK, columns), f32),
            pltpu.VMEM((2, 1, columns), f32),
            pltpu.VMEM((rows, width), f32),
            pltpu.VMEM((2 * chips, rows, width), bf16),
            pltpu.VMEM((slots, width, double), bf16),
            pltpu.VMEM((slots, ff, width), bf16),
            pltpu.VMEM((2, slots * cap, width), bf16),
            pltpu.VMEM((2, slots * cap, 2 * rows), bf16),
            pltpu.VMEM((all_slots, 2 * rows), f32),
            pltpu.VMEM((all_slots, 2 * rows), f32),
            pltpu.VMEM((2, slots * cap, 1), f32),
            pltpu.VMEM((2, 2 * rows, slots * cap), bf16),
            pltpu.VMEM((2 * rows, 2 * rows), bf16),
            pltpu.VMEM((max(chips, requests), 2, rows, width), bf16),
            pltpu.VMEM((max(chips, dp_size - 1), rows, width), bf16),
            pltpu.VMEM((chips + 1, rows, width), bf16),
            pltpu.VMEM((ex_size, all_slots, rows), bf16),
            pltpu.VMEM((all_slots, width), bf16),
            dma((requests,)),
            dma((4,)),
            dma((ring, 2)),
            dma((ex_size - 1,)),
            dma((ex_size - 1,)),
            dma((dp_size - 1,)),
            dma((dp_size - 1,)),
            dma((slots, 2)),
            dma((2, chips, hops)),
            dma((2, chips, hops)),
            dma((chips, hops)),
            dma((chips, hops)),
            dma((chips,)),
            dma((chips,)),
            dma((chips, parts)),
            dma((chips + 1, parts)),
        ],
        compiler_params=pltpu.CompilerParams(
            collective_id=0, has_side_effects=True, vmem_limit_bytes=63 << 20
        ),
        name="layer",
    )(
        past_len, slot_owner, routes_t, pick_t, attn_gain, moe_gain, final_gain, router_t,
        tokens, w_query, w_key, w_value, w_out, cache_keys, cache_values, expert_in, expert_out,
    )


def shards(
    tokens,
    past_len,
    cache_keys,
    cache_values,
    attn_gain,
    w_query,
    w_key,
    w_value,
    w_out,
    moe_gain,
    router,
    expert_in,
    expert_out,
    final_gain,
    slot_owner,
    routes,
    split_pick,
):
    return layer(
        past_len, slot_owner, routes.T, split_pick.T, attn_gain, moe_gain, final_gain, router.T,
        tokens, w_query, w_key, w_value, w_out, cache_keys, cache_values, expert_in, expert_out,
        slot_owner.shape[0], lax.axis_size("dp"), lax.axis_size("expert"),
    )


def solution(mesh):
    return jax.shard_map(
        shards,
        mesh=mesh,
        in_specs=(
            P("expert", None),
            P("expert"),
            P("expert", None, "dp"),
            P("expert", None, "dp"),
            P(),
            P(None, "dp"),
            P(None, "dp"),
            P(None, "dp"),
            P("dp", None),
            P(),
            P(),
            P("expert", None, None),
            P("expert", None, None),
            P(),
            P(),
            P(("expert", "dp"), None),
            P(("expert", "dp"), None),
        ),
        out_specs=P(("expert", "dp"), None),
        check_vma=False,
    )
```

```python
import functools

import jax
import jax.numpy as jnp
from jax import lax
from jax.experimental import pallas as pl
from jax.experimental.pallas import tpu as pltpu
from jax.sharding import PartitionSpec as P

HD = 64
SINK = 4
WINDOW = 4096
MOST = 40
KEY_BLOCK = 512
GROUPS = 3
LAG = 2

epsilon = 1e-05
neg_large = -1e30


def rms_scale(values, gain):
    widened = values.astype(jnp.float32)
    mean_square = jnp.mean(widened * widened, axis=-1, keepdims=True)
    return widened * lax.rsqrt(mean_square + epsilon) * gain


def mm(a, b):
    return jnp.dot(a, b, preferred_element_type=jnp.float32)


def start_if(cond, copy):
    pl.when(cond)(copy.start)


def send(src, dst, send_sem, recv_sem, device):
    return pltpu.make_async_remote_copy(
        src_ref=src,
        dst_ref=dst,
        send_sem=send_sem,
        recv_sem=recv_sem,
        device_id=device,
        device_id_type=pl.DeviceIdType.MESH,
    )


def layer_kernel(
    dp_size, ex_size, len_ref, owner_ref, routes_ref, pick_ref, attn_gain_ref, moe_gain_ref, final_gain_ref,
    router_ref, tok_hbm, wq_hbm, wk_hbm, wv_hbm, wo_hbm, kc_hbm, vc_hbm, win_hbm, wout_hbm,
    out_ref,
    qt_ref, top_ref, total_ref, acc_ref, score_ref, peak_ref,
    stream_ref, all_ref, win_ref, wout_ref, x_ref, sel_ref, gate_ref, rank_ref,
    gcol_ref, back_ref, before_ref, part_ref, sib_ref, land_ref, chosen_ref, slot_router_ref,
    tok_sem, proj_sem, kv_sem, m_send, m_recv, rs_send, rs_recv, w_sem,
    z_send, z_recv, s_send, s_recv, p_send, p_recv, c_send, c_recv,
):
    chips = ex_size // 2
    rows, width = stream_ref.shape
    slots = win_ref.shape[0]
    all_slots = gate_ref.shape[0]
    cap = sel_ref.shape[1] // slots
    ff = wout_ref.shape[1]
    pair = 2 * rows
    hops = z_send.shape[2]
    parts = c_send.shape[1]
    hop_rows, part_rows = rows // hops, rows // parts
    dp, ex = lax.axis_index("dp"), lax.axis_index("expert")
    chip, core = ex // 2, ex % 2
    upper, lower = chip < chips - 1, chip > 0
    sibling = (dp, chip * 2 + 1 - core)
    above = jnp.minimum(chip + 1, chips - 1)
    below = jnp.maximum(chip - 1, 0)
    bf16, f32 = jnp.bfloat16, jnp.float32

    def toward(d):
        return (dp, jnp.where(d == 0, above, below) * 2 + core)

    def weights(s):
        return (
            pltpu.make_async_copy(win_hbm.at[s], win_ref.at[s], w_sem.at[s, 0]),
            pltpu.make_async_copy(wout_hbm.at[s], wout_ref.at[s], w_sem.at[s, 1]),
        )

    peers = [(lax.rem(dp + k, dp_size), ex) for k in range(1, dp_size)]
    peers += [(dp, lax.rem(ex + k, ex_size)) for k in range(1, ex_size)]
    barrier = pltpu.get_barrier_semaphore()
    for peer in peers:
        pl.semaphore_signal(barrier, inc=1, device_id=peer, device_id_type=pl.DeviceIdType.MESH)

    requests, capacity, kv_width = kc_hbm.shape
    q_width = wq_hbm.shape[1]
    heads, kv_local = q_width // HD, kv_width // HD
    share = heads // kv_local
    columns = heads * rows
    group = columns // GROUPS
    blocks = capacity // KEY_BLOCK
    stack = width // KEY_BLOCK
    spans = capacity // width
    ring = win_ref.shape[2] // (2 * kv_width)
    ahead = ring - 2
    proj, pool = win_ref.at[slots - 1], win_ref.at[slots - 2]
    wq_ref = proj.at[:, 0:q_width]
    wk_ref = proj.at[:, q_width : q_width + kv_width]
    wv_ref = proj.at[:, q_width + kv_width : q_width + 2 * kv_width]
    wo_ref = wout_ref.at[slots - 1, 0:q_width]
    half = requests // 2

    def sent(r):
        return part_ref.at[r // 2, r % 2]

    def token(r):
        return part_ref.at[half + r // 2, r % 2]

    def token_copy(r):
        return pltpu.make_async_copy(tok_hbm.at[pl.ds(r * rows, rows)], token(r), tok_sem.at[r])

    proj_copies = [
        pltpu.make_async_copy(src, dst, proj_sem.at[n])
        for n, (src, dst) in enumerate(
            ((wq_hbm, wq_ref), (wk_hbm, wk_ref), (wv_hbm, wv_ref), (wo_hbm, wo_ref))
        )
    ]

    def request_at(step):
        return lax.rem(dp + 1 + step, dp_size)

    def spot(number, which):
        place = lax.rem(number, ring)
        return pl.multiple_of((place * 2 + which) * kv_width, kv_width)

    def block_at(step, i, which):
        row = pl.multiple_of(lax.rem(i, stack) * KEY_BLOCK, KEY_BLOCK)
        column = spot(step * spans + i // stack, which)
        return pl.ds(row, KEY_BLOCK), pl.ds(column, kv_width)

    def kv_copies(number):
        r, span = request_at(number // spans), lax.rem(number, spans)
        here = pl.ds(pl.multiple_of(span * width, width), width)
        place = lax.rem(number, ring)
        return [
            pltpu.make_async_copy(
                src.at[r, here], pool.at[:, pl.ds(spot(number, n), kv_width)], kv_sem.at[place, n]
            )
            for n, src in enumerate((kc_hbm, vc_hbm))
        ]

    for r in range(requests):
        token_copy(r).start()
    for copy in proj_copies:
        copy.start()

    @pl.loop(0, ahead)
    def _(number):
        for copy in kv_copies(number):
            copy.start()

    routes = routes_ref[...]
    lanes = lax.broadcasted_iota(jnp.int32, (1, rows), 1)

    replicas = jnp.zeros(routes.shape, f32)
    for s in range(all_slots):
        owner = owner_ref[s]
        rank_ref[s : s + 1, :rows] = jnp.where(lanes == owner, 1.0, 0.0)
        replicas = replicas + jnp.where(routes == owner, 1.0, 0.0)
    picks = pick_ref[...].astype(f32)
    turn = picks - jnp.floor((picks + 0.5) / replicas) * replicas

    seen = jnp.zeros(routes.shape, f32)
    for s in range(all_slots):
        serving = routes == owner_ref[s]
        hit = jnp.where(serving & (seen == turn), 1.0, 0.0)
        gate_ref[s : s + 1, :rows] = jnp.max(hit, axis=0, keepdims=True)
        seen = seen + jnp.where(serving, 1.0, 0.0)
    chosen_ref[ex] = gate_ref[:, :rows].astype(bf16)
    spots = router_ref.shape[0]
    slot_router_ref[...] = mm(rank_ref[:, :spots].astype(bf16), router_ref[...]).astype(bf16)
    before_ref[...] = jnp.where(
        lax.broadcasted_iota(jnp.int32, (pair, pair), 0)
        < lax.broadcasted_iota(jnp.int32, (pair, pair), 1),
        1.0,
        0.0,
    ).astype(bf16)
    qt_ref[:kv_width] = jnp.zeros((kv_width, columns), bf16)
    gap = lax.broadcasted_iota(jnp.int32, (rows, columns), 0)
    query = lax.broadcasted_iota(jnp.int32, (rows, columns), 1) % rows
    qt_ref[kv_width:] = jnp.where((query > gap) | (gap == rows - 1), neg_large, 0.0).astype(bf16)
    pl.semaphore_wait(barrier, len(peers))

    def masks(k):
        return send(
            chosen_ref.at[ex],
            chosen_ref.at[ex],
            m_send.at[k - 1],
            m_recv.at[k - 1],
            (dp, lax.rem(ex + k, ex_size)),
        )

    def masks_from(k):
        origin = lax.rem(ex + ex_size - k, ex_size)
        return send(
            chosen_ref.at[ex], chosen_ref.at[origin], m_send.at[k - 1], m_recv.at[k - 1], sibling
        )

    for k in range(1, ex_size):
        masks(k).start()

    def weigh(values, weights16):
        return lax.dot_general(
            values, weights16, (((0,), (0,)), ((), ())), preferred_element_type=f32
        )

    def share_out(step):
        return send(
            sent(request_at(step)),
            sib_ref.at[step],
            rs_send.at[step],
            rs_recv.at[step],
            (request_at(step), ex),
        )

    def arrive(number):
        @pl.when(number + ahead < dp_size * spans)
        def _():
            for copy in kv_copies(number + ahead):
                copy.start()

        for copy in kv_copies(number):
            copy.wait()

    for copy in proj_copies:
        copy.wait()
    for r in range(requests):
        token_copy(r).wait()
    group_tokens = part_ref[half : 2 * half].reshape(requests * rows, width)
    normed = rms_scale(group_tokens, attn_gain_ref[...].reshape(1, width)).astype(bf16)
    queries = mm(normed, wq_ref[...]).astype(bf16) * jnp.asarray(HD ** (-0.5), bf16)
    keys_all = mm(normed, wk_ref[...]).astype(bf16)
    values_all = mm(normed, wv_ref[...]).astype(bf16)
    for r in range(requests):
        here = slice(r * rows, (r + 1) * rows)
        x_ref[0, :rows, r * q_width : (r + 1) * q_width] = queries[here]
        x_ref[1, :rows, 2 * r * kv_width : (2 * r + 1) * kv_width] = keys_all[here]
        x_ref[1, :rows, (2 * r + 1) * kv_width : (2 * r + 2) * kv_width] = values_all[here]

    @pl.loop(0, dp_size)
    def _(step):
        r = request_at(step)
        length = len_ref[r]
        arrive(step * spans)
        queries_t = x_ref[0, :rows, pl.ds(pl.multiple_of(r * q_width, q_width), q_width)].T
        for h in range(heads):
            kv = h // share
            qt_ref[kv * HD : (kv + 1) * HD, h * rows : (h + 1) * rows] = queries_t[
                h * HD : (h + 1) * HD, :
            ]
        fresh = pl.multiple_of(r * 2 * kv_width, 2 * kv_width)
        keys_new = x_ref[1, :rows, pl.ds(fresh, kv_width)]
        values_new = x_ref[1, :rows, pl.ds(pl.multiple_of(fresh + kv_width, kv_width), kv_width)]
        scores = mm(keys_new, qt_ref[:kv_width])
        key_pos = lax.broadcasted_iota(jnp.int32, (rows, columns), 0)
        query_pos = lax.broadcasted_iota(jnp.int32, (rows, columns), 1) % rows
        scores = jnp.where(key_pos <= query_pos, scores, neg_large)
        top = jnp.max(scores, axis=0, keepdims=True)
        weights_new = jnp.exp(scores - top)
        top_ref[...] = top
        total_ref[...] = jnp.sum(weights_new, axis=0, keepdims=True)
        acc_ref[...] = weigh(values_new, weights_new.astype(bf16))

        def keys_of(i):
            keys = pool[block_at(step, i, 0)]
            start = i * KEY_BLOCK
            slot_id = lax.broadcasted_iota(jnp.int32, (KEY_BLOCK, rows), 0)
            reach = slot_id + (start - (length - WINDOW + 1))
            mark = jnp.where(slot_id >= length - start, -1, jnp.maximum(reach, -1))
            mark = jnp.where(slot_id < jnp.minimum(length, SINK) - start, rows, mark)
            lane = lax.broadcasted_iota(jnp.int32, (KEY_BLOCK, rows), 1)
            lane = jnp.where(lane == rows - 1, -1, lane)
            hot = jnp.where(mark == lane, 1.0, 0.0).astype(bf16)
            return jnp.concatenate([keys, hot], axis=1)

        def front(keys, buffer, g):
            c = slice(g * group, (g + 1) * group)
            scores = mm(keys, qt_ref[:, c])
            score_ref[buffer, :, c] = scores
            peak_ref[buffer, :, c] = jnp.max(scores, axis=0, keepdims=True)

        def back(i, buffer, g):
            c = slice(g * group, (g + 1) * group)
            values = pool[block_at(step, i, 1)]
            top_old = top_ref[:, c]
            top_new = jnp.maximum(top_old, peak_ref[buffer, :, c])
            factor = jnp.exp(top_old - top_new)
            weights32 = jnp.exp(score_ref[buffer, :, c] - top_new)
            top_ref[:, c] = top_new
            total_ref[:, c] = total_ref[:, c] * factor + jnp.sum(weights32, axis=0, keepdims=True)
            acc_ref[:, c] = acc_ref[:, c] * factor + weigh(values, weights32.astype(bf16))

        keys = keys_of(0)
        for g in range(GROUPS):
            front(keys, 0, g)

        @pl.loop(0, (blocks - 1) // 2)
        def _(pair_id):
            for buffer in range(2):
                i = pair_id * 2 + buffer
                number = step * spans + (i + 1) // stack
                pl.when(lax.rem(i + 1, stack) == 0)(lambda: arrive(number))
                keys = keys_of(i + 1)
                for g in range(GROUPS):
                    front(keys, 1 - buffer, g)
                    back(i, buffer, g)

        if blocks % 2 == 0:
            if (blocks - 1) % stack == 0:
                arrive(step * spans + (blocks - 1) // stack)
            keys = keys_of(blocks - 1)
            for g in range(GROUPS):
                front(keys, 1, g)
                back(blocks - 2, 0, g)
        for g in range(GROUPS):
            back(blocks - 1, (blocks - 1) % 2, g)
        result = acc_ref[...] / total_ref[...]
        pieces = []
        for h in range(heads):
            kv = h // share
            pieces.append(result[kv * HD : (kv + 1) * HD, h * rows : (h + 1) * rows])
        heads_rows = jnp.concatenate(pieces, axis=0).T.astype(bf16)
        sent(r)[...] = mm(heads_rows, wo_ref[...]).astype(bf16)
        pl.when(step < dp_size - 1)(lambda: share_out(step).start())

        share_of = -(-(slots - 2) // (dp_size - 1))

        @pl.when(step < dp_size - 1)
        def _():
            @pl.loop(step * share_of, jnp.minimum((step + 1) * share_of, slots - 2))
            def _(s):
                for copy in weights(s):
                    copy.start()

    attn = sent(dp)[...].astype(f32)
    for step in range(dp_size - 1):
        share_out(step).wait()
        attn = attn + sib_ref[step].astype(f32)
    stream = token(dp)[...].astype(f32) + attn
    stream_ref[...] = stream
    all_ref[chip * 2 + core] = rms_scale(stream, moe_gain_ref[...].reshape(1, width)).astype(bf16)

    def along(d, origin, j):
        block = all_ref.at[origin * 2 + core, pl.ds(j * hop_rows, hop_rows)]
        return send(block, block, z_send.at[d, origin, j], z_recv.at[d, origin, j], toward(d))

    def across(origin, j, owner):
        block = all_ref.at[origin * 2 + owner, pl.ds(j * hop_rows, hop_rows)]
        return send(block, block, s_send.at[origin, j], s_recv.at[origin, j], sibling)

    def halves(origin):
        return send(
            part_ref.at[origin, 1 - core],
            sib_ref.at[origin],
            p_send.at[origin],
            p_recv.at[origin],
            sibling,
        )

    def onward(d, dest, k):
        here = pl.ds(k * part_rows, part_rows)
        arrives = jnp.where((d == 1) & (dest == below), chips, dest)
        return send(
            part_ref.at[dest, core, here],
            land_ref.at[arrives, here],
            c_send.at[dest, k],
            c_recv.at[arrives, k],
            toward(d),
        )

    def landed(place, k):
        here = pl.ds(k * part_rows, part_rows)
        return send(
            part_ref.at[0, core, here],
            land_ref.at[place, here],
            c_send.at[0, k],
            c_recv.at[place, k],
            sibling,
        )

    for j in range(hops):
        start_if(upper, along(0, chip, j))
        start_if(lower, along(1, chip, j))
        across(chip, j, core).start()
    @pl.loop(slots - 2, slots)
    def _(s):
        for copy in weights(s):
            copy.start()

    for k in range(1, ex_size):
        masks_from(k).wait_recv()
        masks(k).wait_send()

    def forward(step, j):
        for d in range(2):
            origin = chip - step if d == 0 else chip + step
            valid = (origin >= 0) & (origin < chips)
            bounded = jnp.clip(origin, 0, chips - 1)

            @pl.when(valid)
            def _():
                along(d, bounded, j).wait_recv()
                across(bounded, j, core).start()

            start_if(valid & (upper if d == 0 else lower), along(d, bounded, j))

    def side_of(step, side):
        origin = chip + (2 * side - 1) * step
        valid = (origin >= 0) & (origin < chips) & ((step > 0) | (side == 0))
        return jnp.clip(origin, 0, chips - 1), valid

    def take(origin, side):
        for j in range(hops):
            across(origin, j, 1 - core).wait_recv()
        block = all_ref[pl.ds(origin * 2, 2)].reshape(pair, width)
        logits = lax.dot_general(
            slot_router_ref[...], block, (((1,), (1,)), ((), ())), preferred_element_type=jnp.float32
        )
        used = jnp.concatenate([chosen_ref[origin * 2], chosen_ref[origin * 2 + 1]], axis=1)
        chosen = used.astype(jnp.float32) > 0.0
        top = jnp.max(jnp.where(chosen, logits, neg_large), axis=0, keepdims=True)
        soft = jnp.where(chosen, jnp.exp(jnp.where(chosen, logits, top) - top), 0.0)
        gate_ref[...] = soft / jnp.sum(soft, axis=0, keepdims=True)
        rank_ref[...] = jnp.where(chosen, mm(used, before_ref[...]), -1.0)
        wanted = lax.broadcasted_iota(jnp.int32, (cap, pair), 0).astype(jnp.float32)
        for s in range(slots):
            row = pl.ds(ex * slots + s, 1)
            mine = wanted == rank_ref[row, :]
            sel_ref[side, s * cap : (s + 1) * cap, :] = jnp.where(mine, 1.0, 0.0).astype(jnp.bfloat16)
            gcol_ref[side, s * cap : (s + 1) * cap, :] = jnp.sum(
                jnp.where(mine, gate_ref[row, :], 0.0), axis=1, keepdims=True
            )
        back_ref[side] = sel_ref[side].T
        for n in range(0, width, 256):
            columns = slice(n, n + 256)
            taken = mm(sel_ref[side], all_ref[pl.ds(origin * 2, 2), :, columns].reshape(pair, 256))
            x_ref[side, :, columns] = taken.astype(jnp.bfloat16)

    def give(origin, side):
        for n in range(0, width, 256):
            columns = slice(n, n + 256)
            spread = mm(back_ref[side], x_ref[side, :, columns])
            part_ref[origin, :, :, columns] = spread.reshape(2, rows, 256).astype(jnp.bfloat16)
        halves(origin).start()

    def combine(step):
        for side in range(2):
            origin, valid = side_of(step, side)

            @pl.when(valid)
            def _():
                halves(origin).wait_recv()
                total = part_ref[origin, core].astype(jnp.float32)
                total = total + sib_ref[origin].astype(jnp.float32)
                part_ref[origin, core] = total.astype(jnp.bfloat16)

            first = chip == 0 if side == 1 else chip == chips - 1

            @pl.when(valid & first & (step > 0))
            def _():
                for k in range(parts):
                    onward(1 - side, origin, k).start()

    def expert(s):
        here = pl.ds(pl.multiple_of(s * cap, cap), cap)
        moe_in = x_ref[:, here, :].reshape(2 * cap, width)
        pieces = []
        for n in range(0, ff, 256):
            g = mm(moe_in, win_ref[s, :, n : n + 256])
            u = mm(moe_in, win_ref[s, :, ff + n : ff + n + 256])
            pieces.append((g / (1.0 + jnp.exp(-g)) * u).astype(bf16))
        activation = jnp.concatenate(pieces, axis=1)
        gate = gcol_ref[:, here, :].reshape(2 * cap, 1)
        for n in range(0, width, 256):
            produced = mm(activation, wout_ref[s, :, n : n + 256]) * gate
            x_ref[:, here, n : n + 256] = produced.astype(bf16).reshape(2, cap, 256)

    @pl.loop(0, chips)
    def _(step):
        @pl.loop(0, 2)
        def _(side):
            origin, valid = side_of(step, side)
            pl.when(valid)(lambda: take(origin, side))

        pl.when(step > 0)(lambda: combine(step - 1))
        busy = side_of(step, 0)[1] | side_of(step, 1)[1]

        @pl.when(busy)
        def _():
            @pl.loop(0, slots // 2)
            def _(couple):
                for s in (couple * 2, couple * 2 + 1):

                    @pl.when(step == 0)
                    def _():
                        for copy in weights(s):
                            copy.wait()

                for s in (couple * 2, couple * 2 + 1):
                    expert(s)
                first = jnp.where(step == 0, (slots // 2 - 1) // 2, 0)
                last = jnp.where(step == 0, slots // 2 - 1, max(slots // 2 - 2, 0))
                pl.when(couple == first)(lambda: forward(step + 1, 0))
                pl.when(couple == last)(lambda: forward(step + 1, 1))

            @pl.loop(0, 2)
            def _(side):
                origin, valid = side_of(step, side)
                pl.when(valid)(lambda: give(origin, side))

    combine(chips - 1)

    turns = (chips - 1) * parts

    @pl.loop(0, turns + LAG)
    def _(turn):
        for which in range(2):
            number = turn - which * LAG
            key, k = 1 + number // parts, lax.rem(number, parts)
            d = jnp.where(chip < chips // 2, which, 1 - which)
            place = jnp.where(d == 0, chip, chips - 1 - chip)
            dest = jnp.where(d == 0, key, chips - 1 - key)

            @pl.when((number >= 0) & (number < turns) & (place > 0) & (key > place))
            def _():
                landed(dest, k).wait_recv()
                here = pl.ds(pl.multiple_of(k * part_rows, part_rows), part_rows)
                total = part_ref[dest, core, here].astype(jnp.float32)
                total = total + land_ref[dest, here].astype(jnp.float32)
                part_ref[dest, core, here] = total.astype(jnp.bfloat16)
                onward(d, dest, k).start()

    for k in range(parts):
        pl.when(lower)(landed(chip, k).wait_recv)
        pl.when(upper)(landed(chips, k).wait_recv)
    total = stream_ref[...] + part_ref[chip, core].astype(jnp.float32)
    total = total + jnp.where(lower, land_ref[chip].astype(jnp.float32), 0.0)
    total = total + jnp.where(upper, land_ref[chips].astype(jnp.float32), 0.0)
    out_ref[...] = rms_scale(total, final_gain_ref[...].reshape(1, width)).astype(jnp.bfloat16)

    @pl.loop(0, chips)
    def _(origin):
        for j in range(hops):
            pl.when(upper & (origin <= chip))(along(0, origin, j).wait_send)
            pl.when(lower & (origin >= chip))(along(1, origin, j).wait_send)
            across(origin, j, core).wait_send()
        halves(origin).wait_send()
        for k in range(parts):
            pl.when(origin > chip)(onward(0, origin, k).wait_send)
            pl.when(origin < chip)(onward(1, origin, k).wait_send)


def layer(
    past_len, slot_owner, routes_t, pick_t, attn_gain, moe_gain, final_gain, router_t,
    tokens, w_query, w_key, w_value, w_out, cache_keys, cache_values, expert_in, expert_out,
    all_slots, dp_size, ex_size,
):
    group_rows, width = tokens.shape
    rows = group_rows // dp_size
    requests, capacity, kv_width = cache_keys.shape
    assert requests == dp_size and rows == 128 and capacity % width == 0 and width % KEY_BLOCK == 0
    chips = ex_size // 2
    slots, _, double = expert_in.shape
    ff = expert_out.shape[1]
    columns = w_query.shape[1] // HD * rows
    cap = 2 * MOST
    hops, parts = 2, 8
    ring = double // (2 * kv_width)
    dma = pltpu.SemaphoreType.DMA
    vmem = pl.BlockSpec(memory_space=pltpu.VMEM)
    smem = pl.BlockSpec(memory_space=pltpu.SMEM)
    hbm = pl.BlockSpec(memory_space=pl.ANY)
    bf16, f32 = jnp.bfloat16, jnp.float32
    return pl.pallas_call(
        functools.partial(layer_kernel, dp_size, ex_size),
        out_shape=jax.ShapeDtypeStruct((rows, width), bf16),
        in_specs=[smem] * 2 + [vmem] * 6 + [hbm] * 9,
        out_specs=vmem,
        scratch_shapes=[
            pltpu.VMEM((2 * kv_width, columns), bf16),
            pltpu.VMEM((1, columns), f32),
            pltpu.VMEM((1, columns), f32),
            pltpu.VMEM((kv_width, columns), f32),
            pltpu.VMEM((2, KEY_BLOCK, columns), f32),
            pltpu.VMEM((2, 1, columns), f32),
            pltpu.VMEM((rows, width), f32),
            pltpu.VMEM((2 * chips, rows, width), bf16),
            pltpu.VMEM((slots, width, double), bf16),
            pltpu.VMEM((slots, ff, width), bf16),
            pltpu.VMEM((2, slots * cap, width), bf16),
            pltpu.VMEM((2, slots * cap, 2 * rows), bf16),
            pltpu.VMEM((all_slots, 2 * rows), f32),
            pltpu.VMEM((all_slots, 2 * rows), f32),
            pltpu.VMEM((2, slots * cap, 1), f32),
            pltpu.VMEM((2, 2 * rows, slots * cap), bf16),
            pltpu.VMEM((2 * rows, 2 * rows), bf16),
            pltpu.VMEM((max(chips, requests), 2, rows, width), bf16),
            pltpu.VMEM((max(chips, dp_size - 1), rows, width), bf16),
            pltpu.VMEM((chips + 1, rows, width), bf16),
            pltpu.VMEM((ex_size, all_slots, rows), bf16),
            pltpu.VMEM((all_slots, width), bf16),
            dma((requests,)),
            dma((4,)),
            dma((ring, 2)),
            dma((ex_size - 1,)),
            dma((ex_size - 1,)),
            dma((dp_size - 1,)),
            dma((dp_size - 1,)),
            dma((slots, 2)),
            dma((2, chips, hops)),
            dma((2, chips, hops)),
            dma((chips, hops)),
            dma((chips, hops)),
            dma((chips,)),
            dma((chips,)),
            dma((chips, parts)),
            dma((chips + 1, parts)),
        ],
        compiler_params=pltpu.CompilerParams(
            collective_id=0, has_side_effects=True, vmem_limit_bytes=63 << 20
        ),
        name="layer",
    )(
        past_len, slot_owner, routes_t, pick_t, attn_gain, moe_gain, final_gain, router_t,
        tokens, w_query, w_key, w_value, w_out, cache_keys, cache_values, expert_in, expert_out,
    )


def shards(
    tokens,
    past_len,
    cache_keys,
    cache_values,
    attn_gain,
    w_query,
    w_key,
    w_value,
    w_out,
    moe_gain,
    router,
    expert_in,
    expert_out,
    final_gain,
    slot_owner,
    routes,
    split_pick,
):
    return layer(
        past_len, slot_owner, routes.T, split_pick.T, attn_gain, moe_gain, final_gain, router.T,
        tokens, w_query, w_key, w_value, w_out, cache_keys, cache_values, expert_in, expert_out,
        slot_owner.shape[0], lax.axis_size("dp"), lax.axis_size("expert"),
    )


def solution(mesh):
    return jax.shard_map(
        shards,
        mesh=mesh,
        in_specs=(
            P("expert", None),
            P("expert"),
            P("expert", None, "dp"),
            P("expert", None, "dp"),
            P(),
            P(None, "dp"),
            P(None, "dp"),
            P(None, "dp"),
            P("dp", None),
            P(),
            P(),
            P("expert", None, None),
            P("expert", None, None),
            P(),
            P(),
            P(("expert", "dp"), None),
            P(("expert", "dp"), None),
        ),
        out_specs=P(("expert", "dp"), None),
        check_vma=False,
    )
```
